32 devices in a mesh: groups: 2 (over y), lat: 8 (over z, x), lon: 2 (over core).
Axes of the slice: x: 2, y: 2, z: 4, core: 2. Of those that a mesh axis runs over, the one named last changes fastest.
Arguments:
- tokens: bfloat16 [16, 256, 768], P(('groups', 'lat'), 'lon'), parts along dimension 0, may hold values from -5 to 5
- gain_attn: float32 [768], replicated, may hold values from 0.25 to 1.75
- w_qkv: bfloat16 [768, 2304], P('lat'), may hold values from -0.048353085 to 0.048353085
- key_bias: bfloat16 [8, 12, 256], P('lat', None, 'lon'), may hold values from -3 to 250
- w_out: bfloat16 [768, 768], P('lat'), may hold values from -0.21875 to 0.21875
- gain_conv: float32 [768], replicated, may hold values from 0.25 to 1.75
- w_conv: bfloat16 [2, 768, 64], replicated, may hold values from -0.75 to 0.75
- lat_taps: float32 [16, 2], replicated, may hold values from -2 to 2
- lon_half: int32 [8], P('lat'), may hold values from 1 to 128, as said below
- lat_half: int32 [8], P('lat'), may hold values from 0 to 1, as said below
- quad_off: int32 [8], P('lat'), may hold values from 0 to 13
Outputs:
- updated: bfloat16 [16, 256, 768], P(('groups', 'lat'), 'lon'), parts along dimension 0
The draws below stay inside these ranges and needn't reach their ends.
There are 2 independent parts, one for each index of `groups`. The reference program is written for one: setup_inputs(seed, part) draws one part's arguments, and reference() takes and returns one part's arrays. A program takes and returns all parts, laid end to end along the dimension named above; an argument that names none is the same for every part. Nothing has to cross between parts.
Inputs may be any that keep to these rules, and one draw needn't show every extreme that they name: `lon_half`: the bands at either pole reach 128. `lat_half`: both polar bands have 1.
All inputs are finite; a program needn't handle non-finite values.
Results may differ from the reference program's by a relative error of at most 0.008.
Values may be sent and summed in bfloat16 or wider, within the bound.
A program may use at most 64 MiB of HBM per device.

```python
import math
import jax
import jax.numpy as jnp
from jax import lax

D = 768
H = 12
DH = 64
GW = 64
KB = 2
TAPS = 16
NLON = 256
NLAT = 8


def draw_tokens(key, part):
    col_key, main_key, base_key, wave_key = jax.random.split(key, 4)
    lon_angle = 2.0 * math.pi / NLON * jnp.arange(NLON, dtype=jnp.float32)
    first_cos = jnp.cos(lon_angle)[None, :, None]
    first_sin = jnp.sin(lon_angle)[None, :, None]
    wave_coef = jax.random.normal(wave_key, (4, NLAT, 1, D), jnp.float32)
    col_scale = jnp.exp(jax.random.uniform(col_key, (D,), jnp.float32, math.log(0.2), math.log(2.0)))
    rough_part = jnp.clip(jax.random.normal(main_key, (NLAT, NLON, D), jnp.float32), -3.0, 3.0) * col_scale
    base_part = 0.9 * jax.random.normal(base_key, (NLAT, 1, D), jnp.float32)
    smooth_part = 0.4 * (wave_coef[0] * first_cos + wave_coef[1] * first_sin)
    values = rough_part + base_part + smooth_part
    return jnp.clip(values, -5.0, 5.0).astype(jnp.bfloat16)


def draw_w_qkv(key, part):
    sign_key, size_key = jax.random.split(jax.random.fold_in(key, 23), 2)
    sign_flip = 2.0 * jax.random.randint(sign_key, (D, 3 * D), 0, 2).astype(jnp.float32) - 1.0
    jitter = jax.random.uniform(size_key, (D, 3 * D), jnp.float32, 1.1, 1.3)
    return (sign_flip * jitter * float(D) ** (-0.5)).astype(jnp.bfloat16)


def draw_key_bias(key, part):
    base_key = jax.random.fold_in(key, 0)
    values = jnp.clip(0.6 * jax.random.normal(base_key, (NLAT, H, NLON), jnp.float32), -3.0, 3.0)
    return values.astype(jnp.bfloat16)


def draw_lat_taps(key, part):
    sign_key, size_key = jax.random.split(key)
    sign_flip = 2.0 * jax.random.randint(sign_key, (TAPS, KB), 0, 2).astype(jnp.float32) - 1.0
    magnitude = jax.random.uniform(size_key, (TAPS, KB), jnp.float32, 0.8, 2.0)
    return sign_flip * magnitude


def draw_lon_half(key, part):
    factor = jax.random.randint(key, (NLAT,), 4, 8)
    band_ids = jnp.arange(NLAT, dtype=jnp.int32)
    from_pole = jnp.minimum(band_ids, NLAT - 1 - band_ids)
    widths = factor * NLON * NLAT // (128 * (2 * from_pole + 1))
    widths = jnp.where(from_pole == 0, NLON // 2, widths)
    return jnp.clip(widths, 1, NLON // 2)


def draw_lat_half(key, part):
    pick_key, zero_key = jax.random.split(jax.random.fold_in(key, 11))
    picked = jax.random.randint(pick_key, (NLAT,), 0, 2)
    band_ids = jnp.arange(NLAT, dtype=jnp.int32)
    centre = NLAT // 2
    near_centre = jnp.abs(band_ids - centre) <= 1
    zero_band = jax.random.randint(zero_key, (), 1, NLAT - 4)
    zero_band = jnp.where(zero_band >= centre - 1, zero_band + 3, zero_band)
    picked = jnp.where(near_centre, 1, picked)
    picked = jnp.where(band_ids == zero_band, 0, picked)
    at_pole = (band_ids == 0) | (band_ids == NLAT - 1)
    return jnp.where(at_pole, 1, picked)


def set_ends(values, rng, least, top_value):
    longest = values.shape.index(max(values.shape))
    spots = []
    for shift in (0, 1):
        where = [jax.random.randint(jax.random.fold_in(rng, axis), (), 0, length) for axis, length in enumerate(values.shape)]
        where[longest] = (where[longest] + shift) % values.shape[longest]
        spots.append(tuple(where))
    return values.at[spots[0]].set(least).at[spots[1]].set(top_value)


def level_of(own_key, dims, pieces, least, high):
    def one(dim, blocks):
        draws = jax.random.uniform(jax.random.fold_in(jax.random.fold_in(own_key, 6), dim), (blocks,), jnp.float32, least / len(pieces), high / len(pieces))
        return jnp.repeat(jnp.exp(draws), dims[dim] // blocks).reshape((-1,) + (1,) * (len(dims) - dim - 1))

    loudness = one(*pieces[0])
    for cut in pieces[1:]:
        loudness = loudness * one(*cut)
    return loudness


def normal_values(stream_key, shape, width, most, cuts=(), held_as=jnp.bfloat16):
    level = level_of(stream_key, shape, cuts, -0.22, 0.18) if cuts else 1.0
    drawn = jax.random.normal(stream_key, shape, jnp.float32) * width * level
    return jnp.minimum(jnp.maximum(drawn, -most), most).astype(held_as)


def setup_inputs(seed: int = 0, part: int = 0) -> dict:
    arg_keys = jax.random.split(jax.random.key(seed), 12)
    part_keys = jax.random.split(jax.random.fold_in(arg_keys[11], part), 12)
    tokens = draw_tokens(jax.random.fold_in(jax.random.fold_in(arg_keys[11], part), 71), part)
    gain_attn = jnp.clip(1.0 + 0.15 * jax.random.normal(arg_keys[1], (D,), jnp.float32), 0.25, 1.75)
    w_qkv = draw_w_qkv(jax.random.fold_in(arg_keys[11], 71), part)
    key_bias = draw_key_bias(jax.random.fold_in(arg_keys[11], 71), part)
    w_out = normal_values(arg_keys[4], (D, D), D ** -0.5, 0.21875, ((0, 8),))
    gain_conv = jnp.clip(1.0 + 0.15 * jax.random.normal(arg_keys[5], (D,), jnp.float32), 0.25, 1.75)
    w_conv = normal_values(arg_keys[6], (KB, D, GW), GW ** -0.5, 0.75)
    lat_taps = draw_lat_taps(jax.random.fold_in(arg_keys[11], 71), part)
    lon_half = draw_lon_half(jax.random.fold_in(arg_keys[11], 71), part)
    lat_half = draw_lat_half(jax.random.fold_in(arg_keys[11], 71), part)
    quad_off = set_ends(jax.random.randint(arg_keys[10], (NLAT,), 0, TAPS - 2), jax.random.fold_in(arg_keys[10], 1), 0, (TAPS - 2) - 1).astype(jnp.int32)
    return dict(tokens=tokens, gain_attn=gain_attn, w_qkv=w_qkv, key_bias=key_bias, w_out=w_out, gain_conv=gain_conv, w_conv=w_conv, lat_taps=lat_taps, lon_half=lon_half, lat_half=lat_half, quad_off=quad_off)


def layer_norm(inputs, gain):
    values = inputs.astype(jnp.float32)
    average = lax.optimization_barrier(jnp.mean(values, axis=-1, keepdims=True))
    centered = values - average
    variance = lax.optimization_barrier(jnp.mean(centered * centered, axis=-1, keepdims=True))
    return centered * lax.rsqrt(variance + 1e-05) * gain

def group_mix(inputs, w_conv):
    basis, length, channels = inputs.shape
    group_width = w_conv.shape[2]
    groups = channels // group_width
    mixed_rows = jnp.einsum('kjgc,kgce->kjge', inputs.reshape(basis, length, groups, group_width).astype(jnp.float32), w_conv.reshape(basis, groups, group_width, group_width).astype(jnp.float32))
    return mixed_rows.reshape(basis, length, channels).astype(jnp.bfloat16)

def lon_weights(row_ids, col_ids, half_width, lon_total):
    offset_lon = jnp.mod(col_ids[None, :] - row_ids[:, None] + lon_total // 2, lon_total) - lon_total // 2
    distance = jnp.abs(offset_lon).astype(jnp.float32)
    span_plus = (half_width + 1).astype(jnp.float32)
    tent_weight = jnp.where(distance <= half_width.astype(jnp.float32), (1.0 - distance / span_plus) / span_plus, 0.0)
    odd_weight = tent_weight * offset_lon.astype(jnp.float32) / span_plus
    return jnp.stack([tent_weight, odd_weight]).astype(jnp.bfloat16)

def reference(tokens, gain_attn, w_qkv, key_bias, w_out, gain_conv, w_conv, lat_taps, lon_half, lat_half, quad_off):
    score_scale = DH ** (-0.5)

    def attend_row(inputs):
        band_tokens, band_bias = inputs
        normed = layer_norm(band_tokens, gain_attn).astype(jnp.bfloat16)
        projected = jnp.dot(normed, w_qkv, preferred_element_type=jnp.float32).astype(jnp.bfloat16)
        queries = projected[:, :D].reshape(NLON, H, DH).astype(jnp.float32)
        key_rows = projected[:, D:2 * D].reshape(NLON, H, DH).astype(jnp.float32)
        value_rows = projected[:, 2 * D:].reshape(NLON, H, DH).astype(jnp.float32)
        scores = jnp.einsum('qhd,khd->hqk', queries, key_rows) * score_scale + band_bias.astype(jnp.float32)[:, None, :]
        exp_scores = jnp.exp(scores - lax.optimization_barrier(jnp.max(scores, axis=-1, keepdims=True)))
        totals = lax.optimization_barrier(jnp.sum(exp_scores, axis=-1))
        weighted = jnp.einsum('hqk,khd->qhd', exp_scores.astype(jnp.bfloat16).astype(jnp.float32), value_rows)
        attended = (weighted / totals.T[:, :, None]).reshape(NLON, D).astype(jnp.bfloat16)
        return (band_tokens.astype(jnp.float32) + jnp.dot(attended, w_out, preferred_element_type=jnp.float32)).astype(jnp.bfloat16)
    middle = lax.map(attend_row, (tokens, key_bias))
    conv_in = lax.map(lambda band_rows: layer_norm(band_rows, gain_conv).astype(jnp.bfloat16), middle)
    zero_row = jnp.zeros((1, NLON, D), jnp.bfloat16)
    padded = jnp.concatenate([zero_row, conv_in, zero_row], axis=0)
    offsets = jnp.arange(3, dtype=jnp.int32) - 1
    lon_ids = jnp.arange(NLON, dtype=jnp.int32)

    def conv_row(band_index):
        stacked = lax.dynamic_slice_in_dim(padded, band_index, 3, 0)
        tap_vals = lat_taps[quad_off[band_index] + offsets + 1]
        tap_vals = jnp.where((jnp.abs(offsets) <= lat_half[band_index])[:, None], tap_vals, 0.0)
        summed = jnp.einsum('rk,rjd->kjd', tap_vals, stacked.astype(jnp.float32), precision=lax.Precision.HIGHEST).astype(jnp.bfloat16)
        own_row = lax.dynamic_index_in_dim(conv_in, band_index, 0, keepdims=False)
        pole_gain = jnp.where(band_index == 0, tap_vals[0], 0.0) + jnp.where(band_index == NLAT - 1, tap_vals[2], 0.0)
        pole_rows = (pole_gain[:, None, None] * own_row.astype(jnp.float32)[None]).astype(jnp.bfloat16)
        mixed_rows = group_mix(summed, w_conv)
        pole_mixed = group_mix(pole_rows, w_conv)
        blended = (mixed_rows.astype(jnp.float32) + jnp.roll(pole_mixed, -(NLON // 2), axis=1).astype(jnp.float32)).astype(jnp.bfloat16)
        coeffs = lon_weights(lon_ids, lon_ids, lon_half[band_index], NLON)
        conv_out = jnp.einsum('kjc,kcd->jd', coeffs.astype(jnp.float32), blended.astype(jnp.float32))
        own_mid = lax.dynamic_index_in_dim(middle, band_index, 0, keepdims=False)
        return (own_mid.astype(jnp.float32) + conv_out).astype(jnp.bfloat16)
    return lax.map(conv_row, jnp.arange(NLAT, dtype=jnp.int32))
```

```python
import jax
import jax.numpy as jnp
from jax import lax
from jax.experimental import pallas as pl
from jax.experimental.pallas import tpu as pltpu
from jax.sharding import PartitionSpec as P


def padded(cells, sides, width):
    for axis, dim in sides:
        count = lax.axis_size(axis)
        ends = count - 1
        head = lax.slice_in_dim(cells, 0, width, axis=dim)
        tail = lax.slice_in_dim(cells, cells.shape[dim] - width, cells.shape[dim], axis=dim)
        cells = jnp.concatenate(
            [
                lax.ppermute(tail, axis, [(i, (i + 1) % count) for i in range(ends)]),
                cells,
                lax.ppermute(head, axis, [((i + 1) % count, i) for i in range(ends)]),
            ],
            axis=dim,
        )
    return cells


def layer_norm(inputs, gain):
    values = inputs.astype(jnp.float32)
    average = jnp.mean(values, axis=-1, keepdims=True)
    centered = values - average
    variance = jnp.mean(centered * centered, axis=-1, keepdims=True)
    return centered * lax.rsqrt(variance + 1e-05) * gain


def group_mix(inputs, w_conv):
    basis, length, channels = inputs.shape
    group_width = w_conv.shape[2]
    groups = channels // group_width
    mixed_rows = jnp.einsum(
        "kjgc,kgce->kjge",
        inputs.reshape(basis, length, groups, group_width),
        w_conv.reshape(basis, groups, group_width, group_width),
        preferred_element_type=jnp.float32,
    )
    return mixed_rows.reshape(basis, length, channels).astype(jnp.bfloat16)


def lon_weights(row_ids, col_ids, half_width, lon_total):
    offset_lon = (
        jnp.mod(col_ids[None, :] - row_ids[:, None] + lon_total // 2, lon_total) - lon_total // 2
    )
    distance = jnp.abs(offset_lon).astype(jnp.float32)
    span_plus = (half_width + 1).astype(jnp.float32)
    tent_weight = jnp.where(
        distance <= half_width.astype(jnp.float32), (1.0 - distance / span_plus) / span_plus, 0.0
    )
    odd_weight = tent_weight * offset_lon.astype(jnp.float32) / span_plus
    return jnp.stack([tent_weight, odd_weight]).astype(jnp.bfloat16)


def start_state(query_count, head_count, head_dim):
    running_max = jnp.full((head_count, query_count), -jnp.inf, jnp.float32)
    running_sum = jnp.zeros((head_count, query_count), jnp.float32)
    running_out = jnp.zeros((query_count, head_count, head_dim), jnp.float32)
    return (running_max, running_sum, running_out)


def attend_keys(carry_state, queries, key_rows, value_rows, bias_rows, score_scale):
    key_count = key_rows.shape[0]
    for offset in range(0, key_count, 128):
        running_max, running_sum, running_out = carry_state
        key_block = key_rows[offset : offset + 128]
        value_block = value_rows[offset : offset + 128]
        bias_block = bias_rows[offset : offset + 128]
        scores = (
            jnp.einsum("qhd,khd->hqk", queries, key_block, preferred_element_type=jnp.float32)
            * score_scale
        )
        scores = scores + bias_block.T.astype(jnp.float32)[:, None, :]
        new_max = jnp.maximum(running_max, jnp.max(scores, axis=-1))
        rescale = jnp.exp(running_max - new_max)
        exp_scores = jnp.exp(scores - new_max[:, :, None])
        running_sum = running_sum * rescale + jnp.sum(exp_scores, axis=-1)
        running_out = running_out * rescale.T[:, :, None] + jnp.einsum(
            "hqk,khd->qhd",
            exp_scores.astype(jnp.bfloat16),
            value_block,
            preferred_element_type=jnp.float32,
        )
        carry_state = (new_max, running_sum, running_out)
    return carry_state


def finish_state(carry_state):
    running_max, running_sum, running_out = carry_state
    finished = running_out / running_sum.T[:, :, None]
    return finished.reshape(finished.shape[0], -1).astype(jnp.bfloat16)


def lon_conv(blended, half_width, first_col, out_cols):
    lon_total = blended.shape[1]
    block_cols = min(128, lon_total)
    block_count = lon_total // block_cols
    first_block = jnp.floor_divide(first_col - half_width, block_cols)
    last_block = jnp.floor_divide(first_col + out_cols - 1 + half_width, block_cols)
    turn_count = jnp.minimum(block_count, last_block - first_block + 1)
    row_ids = first_col + jnp.arange(out_cols, dtype=jnp.int32)

    def add_block(turn_index, running_out):
        block_at = jnp.mod(first_block + turn_index, block_count)
        lon_block = lax.dynamic_slice_in_dim(blended, block_at * block_cols, block_cols, 1)
        col_ids = block_at * block_cols + jnp.arange(block_cols, dtype=jnp.int32)
        coeffs = lon_weights(row_ids, col_ids, half_width, lon_total)
        return running_out + jnp.einsum(
            "kjc,kcd->jd", coeffs, lon_block, preferred_element_type=jnp.float32
        )

    initial = jnp.zeros((out_cols, blended.shape[2]), jnp.float32)
    return lax.fori_loop(0, turn_count, add_block, initial)


def per_device(
    tokens,
    gain_attn,
    w_qkv,
    key_bias,
    w_out,
    gain_conv,
    w_conv,
    lat_taps,
    lon_half,
    lat_half,
    quad_off,
):
    own_tokens = tokens[0]
    count_lon, model_width = own_tokens.shape
    head_count = key_bias.shape[1]
    head_dim = model_width // head_count
    score_scale = head_dim ** (-0.5)
    lon_place = lax.axis_index("lon")
    normed = layer_norm(own_tokens, gain_attn).astype(jnp.bfloat16)
    bias_rows = key_bias[0].T
    full_qkv, full_out = (
        lax.all_gather(w_qkv, "lat", axis=0, tiled=True),
        lax.all_gather(w_out, "lat", axis=0, tiled=True),
    )
    projected = jnp.dot(normed, full_qkv, preferred_element_type=jnp.float32).astype(jnp.bfloat16)
    queries = projected[:, :model_width].reshape(count_lon, head_count, head_dim)
    key_here = projected[:, model_width : 2 * model_width]
    value_here = projected[:, 2 * model_width :]
    key_piece = lax.all_gather(key_here, "lon", axis=0, tiled=True)
    value_piece = lax.all_gather(value_here, "lon", axis=0, tiled=True)
    bias_piece = lax.all_gather(bias_rows, "lon", axis=0, tiled=True)
    length = key_piece.shape[0]
    carry_state = attend_keys(
        start_state(count_lon, head_count, head_dim),
        queries,
        key_piece.reshape(length, head_count, head_dim),
        value_piece.reshape(length, head_count, head_dim),
        bias_piece,
        score_scale,
    )
    attended = finish_state(carry_state)
    branch_out = jnp.dot(attended, full_out, preferred_element_type=jnp.float32)
    middle = (own_tokens.astype(jnp.float32) + branch_out).astype(jnp.bfloat16)
    conv_in = layer_norm(middle, gain_conv).astype(jnp.bfloat16)
    stacked = padded(conv_in[None], (("lat", 0),), 1)
    lat_row = lax.axis_index("lat")
    last_band = lax.axis_size("lat") - 1
    offsets = jnp.arange(3, dtype=jnp.int32) - 1
    one_hot = (
        (quad_off[0] + offsets + 1)[:, None]
        == jnp.arange(lat_taps.shape[0], dtype=jnp.int32)[None, :]
    ).astype(jnp.float32)
    tap_vals = jnp.dot(one_hot, lat_taps, precision=lax.Precision.HIGHEST)
    tap_vals = jnp.where((jnp.abs(offsets) <= lat_half[0])[:, None], tap_vals, 0.0)
    summed = jnp.einsum(
        "rk,rjd->kjd", tap_vals, stacked.astype(jnp.float32), precision=lax.Precision.HIGHEST
    ).astype(jnp.bfloat16)
    pole_gain = jnp.where(lat_row == 0, tap_vals[0], 0.0) + jnp.where(
        lat_row == last_band, tap_vals[2], 0.0
    )
    first_col = lon_place * count_lon
    pole_rows = (pole_gain[:, None, None] * conv_in.astype(jnp.float32)[None]).astype(jnp.bfloat16)
    mixed_rows = group_mix(summed, w_conv)
    pole_mixed = group_mix(pole_rows, w_conv)
    circle_rows, pole_all = (
        lax.all_gather(mixed_rows, "lon", axis=1, tiled=True),
        lax.all_gather(pole_mixed, "lon", axis=1, tiled=True),
    )
    lon_total = circle_rows.shape[1]
    blended = (
        circle_rows.astype(jnp.float32)
        + jnp.roll(pole_all, -(lon_total // 2), axis=1).astype(jnp.float32)
    ).astype(jnp.bfloat16)
    conv_out = lon_conv(blended, lon_half[0], first_col, count_lon)
    return (middle.astype(jnp.float32) + conv_out).astype(jnp.bfloat16)[None]


BF = jnp.bfloat16
F32 = jnp.float32
MESH = pl.DeviceIdType.MESH


def norm_rows(values, gain):
    values = values.astype(F32)
    average = jnp.mean(values, axis=-1, keepdims=True)
    centered = values - average
    variance = jnp.mean(centered * centered, axis=-1, keepdims=True)
    return (centered * lax.rsqrt(variance + 1e-05) * gain).astype(BF)


def fused_kernel(
    nx, nz,
    lat_taps, lon_half, lat_half, quad_off,
    tokens, gain_attn, w_qkv, key_bias, w_out, gain_conv, w_conv,
    out,
    wq, wo, tok, normed, bias, bias_f, att_out, att_in, halo, other_in, mixer, mixed_all, middle,
    q_send, q_recv, o_send, o_recv, r_send, r_recv, t_send, t_recv, a_send, a_recv, h_send, h_recv,
):
    y, place, c = lax.axis_index("groups"), lax.axis_index("lat"), lax.axis_index("lon")
    z, x = lax.div(place, nx), lax.rem(place, nx)
    quad = y * 2 + c
    x_peer = (y, z * nx + (1 - x), c)
    z_up, z_down = (y, place + nx, c), (y, place - nx, c)
    sibling = (y, place, 1 - c)
    y_peer = (1 - y, place, c)
    diagonal = (1 - y, place, 1 - c)
    band_up, band_down = (y, place + 1, c), (y, place - 1, c)
    has_up, has_down = z < nz - 1, z > 0
    cross_up = jnp.logical_and(x == 1, has_up)
    cross_down = jnp.logical_and(x == 0, has_down)
    lat_count = nx * nz
    shard = w_qkv.shape[0]
    width = tokens.shape[1]
    rows = tokens.shape[0]
    head = 64
    part = width // 4
    half = width // 2

    barrier = pltpu.get_barrier_semaphore()

    def greet(device):
        pl.semaphore_signal(barrier, inc=1, device_id=device, device_id_type=MESH)

    for device in (x_peer, sibling, y_peer, diagonal):
        greet(device)
    for cond, device in (
        (has_up, z_up), (has_down, z_down), (cross_up, band_up), (cross_down, band_down)
    ):
        @pl.when(cond)
        def _(device=device):
            greet(device)

    for pick in range(4):
        @pl.when(quad == pick)
        def _(pick=pick):
            wq[pl.ds(place * shard, shard), :] = jnp.concatenate(
                [w_qkv[:, j * width + pick * part : j * width + (pick + 1) * part] for j in range(3)],
                axis=1,
            )
    tok[y, pl.ds(c * rows, rows), :] = tokens[...]
    bias[c] = key_bias[...]
    wo[pl.ds(place * shard, shard), :] = w_out[...]

    pl.semaphore_wait(
        barrier,
        4 + has_up.astype(jnp.int32) + has_down.astype(jnp.int32)
        + cross_up.astype(jnp.int32) + cross_down.astype(jnp.int32),
    )

    def remote(source, target, send, recv, device):
        return pltpu.make_async_remote_copy(
            src_ref=source, dst_ref=target, send_sem=send, recv_sem=recv,
            device_id=device, device_id_type=MESH,
        )

    def q_at(slot):
        return wq.at[pl.ds(slot * shard, shard), :]

    def o_at(slot):
        return wo.at[pl.ds(slot * shard, shard), pl.ds(c * half, half)]

    def o_other(slot):
        return wo.at[pl.ds(slot * shard, shard), pl.ds((1 - c) * half, half)]

    class Gather:
        def __init__(self, at, send, recv, relay):
            self.at, self.send, self.recv, self.relay = at, send, recv, relay

        def copy(self, slot, k, way, device):
            return remote(self.at(slot), self.at(slot), self.send.at[k, way], self.recv.at[slot], device)

        def hop(self, slot, k):
            return remote(self.at(slot), self.at(slot), r_send.at[k], r_recv.at[slot], sibling)

        def own(self, act):
            act(self.copy(place, 0, 0, x_peer))

            @pl.when(has_up)
            def _():
                act(self.copy(place, 0, 1, z_up))

            @pl.when(has_down)
            def _():
                act(self.copy(place, 0, 2, z_down))

        def step(self, t, receive):
            act = (lambda d: d.start()) if receive else (lambda d: d.wait_send())
            for sign, reach, onward, device, way, k in (
                (-1, z >= t, has_up, z_up, 1, t),
                (1, z + t <= nz - 1, has_down, z_down, 2, nz - 1 + t),
            ):
                slot = (z + sign * t) * nx + x

                @pl.when(reach)
                def _(slot=slot, k=k):
                    if receive:
                        self.copy(slot, k, 0, x_peer).wait_recv()
                    act(self.copy(slot, k, 0, x_peer))

                @pl.when(jnp.logical_and(reach, onward))
                def _(slot=slot, k=k, way=way, device=device):
                    act(self.copy(slot, k, way, device))

                if self.relay:
                    @pl.when(reach)
                    def _(slot=slot, k=k):
                        act(self.hop(slot, k))

        def across(self):
            for zz in range(nz):
                slot = zz * nx + (1 - x)
                self.copy(slot, 0, 0, x_peer).wait_recv()
                if self.relay:
                    self.hop(slot, 2 * nz - 1 + zz).start()

        def finish(self):
            self.own(lambda d: d.wait_send())
            for t in range(1, nz):
                self.step(t, False)
            if self.relay:
                for zz in range(nz):
                    slot = zz * nx + (1 - x)
                    self.hop(slot, 2 * nz - 1 + zz).wait_send()

    gather_q = Gather(q_at, q_send, q_recv, False)
    gather_o = Gather(o_at, o_send, o_recv, True)
    start = lambda d: d.start()

    gather_q.own(start)

    def tok_at(yy, cc):
        return tok.at[yy, pl.ds(cc * rows, rows), :]

    tok_copies = [
        remote(tok_at(y, c), tok_at(y, c), t_send.at[0], t_recv.at[0], y_peer),
        remote(tok_at(y, c), tok_at(y, c), t_send.at[1], t_recv.at[1], sibling),
        remote(tok_at(1 - y, c), tok_at(1 - y, c), t_send.at[2], t_recv.at[2], sibling),
        remote(bias.at[c], bias.at[c], t_send.at[3], t_recv.at[3], sibling),
    ]
    for k in (0, 1, 3):
        tok_copies[k].start()

    gain_a = gain_attn[...]

    def norm_block(yy, cc):
        normed[yy, pl.ds(cc * rows, rows), :] = norm_rows(tok[yy, pl.ds(cc * rows, rows), :], gain_a)

    norm_block(y, c)
    pair_row = lax.broadcasted_iota(jnp.int32, (width, 2 * head), 0)
    pair_col = lax.broadcasted_iota(jnp.int32, (width, 2 * head), 1)
    same = lax.rem(lax.div(pair_row, head), 2) == lax.div(pair_col, head)
    for b in range(2):
        wide = jnp.concatenate([w_conv[b], w_conv[b]], axis=1).astype(F32)
        mixer[b] = jnp.where(same, wide, 0.0).astype(BF)

    gather_q.step(1, True)
    tok_copies[1].wait_recv()
    norm_block(y, 1 - c)
    tok_copies[0].wait_recv()
    tok_copies[2].start()
    gather_q.step(2, True)
    norm_block(1 - y, c)
    gather_o.own(start)
    tok_copies[2].wait_recv()
    norm_block(1 - y, 1 - c)
    gather_q.step(3, True)
    tok_copies[3].wait_recv()
    bias_f[...] = jnp.concatenate([bias[0], bias[1]], axis=1).astype(F32)
    gather_q.across()
    gather_o.step(1, True)

    def att_copy(r, to_c, k, device):
        return remote(
            att_out.at[r, pl.ds(to_c * rows, rows), :], att_in.at[quad],
            a_send.at[k], a_recv.at[quad], device,
        )

    att_copies = [
        att_copy(0, c, 0, y_peer), att_copy(0, 1 - c, 1, diagonal), att_copy(1, 1 - c, 2, sibling)
    ]

    def attend(sample, r, between):
        projected = jnp.dot(normed[sample], wq[...], preferred_element_type=F32).astype(BF)
        between()
        pieces = []
        for h in range(3):
            queries = projected[:, h * head : (h + 1) * head] * jnp.asarray(head ** -0.5, BF)
            keys = projected[:, part + h * head : part + (h + 1) * head]
            vals = projected[:, 2 * part + h * head : 2 * part + (h + 1) * head]
            scores = lax.dot_general(
                queries, keys, (((1,), (1,)), ((), ())), preferred_element_type=F32
            ) + bias_f[pl.ds(quad * 3 + h, 1), :]
            expd = jnp.exp(scores - jnp.max(scores, axis=-1, keepdims=True))
            totals = jnp.sum(expd, axis=-1, keepdims=True)
            pieces.append(jnp.dot(expd.astype(BF), vals, preferred_element_type=F32) / totals)
        att_out[r] = jnp.concatenate(pieces, axis=1).astype(BF)

    attend(1 - y, 0, lambda: gather_o.step(2, True))
    att_copies[0].start()
    att_copies[1].start()
    gather_o.step(3, True)
    attend(y, 1, gather_o.across)
    att_copies[2].start()
    att_in[quad] = att_out[1, pl.ds(c * rows, rows), :]

    for t in range(1, nz):
        for sign, reach in ((-1, z >= t), (1, z + t <= nz - 1)):
            @pl.when(reach)
            def _(slot=(z + sign * t) * nx + x):
                remote(o_other(slot), o_other(slot), r_send.at[0], r_recv.at[slot], sibling).wait_recv()
    for zz in range(nz):
        slot = zz * nx + (1 - x)
        remote(o_other(slot), o_other(slot), r_send.at[0], r_recv.at[slot], sibling).wait_recv()
    for source in (y * 2 + (1 - c), (1 - y) * 2 + c, (1 - y) * 2 + (1 - c)):
        remote(att_in.at[source], att_in.at[source], a_send.at[0], a_recv.at[source], sibling).wait_recv()
    branch = tokens[...].astype(F32)
    for p in range(4):
        branch = branch + jnp.dot(
            att_in[p], wo[p * part : (p + 1) * part, :], preferred_element_type=F32
        )
    mid = branch.astype(BF)
    middle[...] = mid
    conv_in = norm_rows(mid, gain_conv[...])
    halo[1] = conv_in

    inner_up, inner_down = place < lat_count - 1, place > 0
    to_up = remote(halo.at[1], halo.at[0], h_send.at[0], h_recv.at[0], band_up)
    to_down = remote(halo.at[1], halo.at[2], h_send.at[1], h_recv.at[1], band_down)
    to_side = remote(halo.at[1], other_in, h_send.at[2], h_recv.at[2], sibling)

    @pl.when(inner_up)
    def _():
        to_up.start()

    @pl.when(inner_down)
    def _():
        to_down.start()

    to_side.start()

    @pl.when(jnp.logical_not(inner_down))
    def _():
        halo[0] = jnp.zeros((rows, width), BF)

    @pl.when(jnp.logical_not(inner_up))
    def _():
        halo[2] = jnp.zeros((rows, width), BF)

    base = quad_off[0]
    reach_lat = lat_half[0]
    wide_ok = reach_lat >= 1
    taps = [
        [
            lat_taps[base + r, b] if r == 1 else jnp.where(wide_ok, lat_taps[base + r, b], 0.0)
            for b in range(2)
        ]
        for r in range(3)
    ]
    span = (lon_half[0] + 1).astype(F32)
    limit = lon_half[0].astype(F32)
    diff = lax.broadcasted_iota(jnp.int32, (rows, rows), 1) - lax.broadcasted_iota(
        jnp.int32, (rows, rows), 0
    )

    def coeffs(offset):
        offset = offset.astype(F32)
        distance = jnp.abs(offset)
        tent = jnp.where(distance <= limit, (1.0 - distance / span) / span, 0.0)
        odd = tent * offset / span
        return jnp.concatenate([tent.astype(BF), odd.astype(BF)], axis=1)

    own_coeffs = coeffs(diff)
    side_coeffs = coeffs(jnp.where(diff >= 0, diff - rows, diff + rows))

    def mix(values, b):
        return jnp.concatenate(
            [
                jnp.dot(
                    values[:, p * 2 * head : (p + 1) * 2 * head],
                    mixer[b, p * 2 * head : (p + 1) * 2 * head, :],
                    preferred_element_type=F32,
                )
                for p in range(width // (2 * head))
            ],
            axis=1,
        ).astype(BF)

    to_side.wait_recv()
    side_rows = other_in[...].astype(F32)
    polar = []
    for b in range(2):
        gain = jnp.where(place == 0, taps[0][b], 0.0) + jnp.where(
            place == lat_count - 1, taps[2][b], 0.0
        )
        polar.append(mix((gain * side_rows).astype(BF), b))

    @pl.when(inner_down)
    def _():
        to_up.wait_recv()

    @pl.when(inner_up)
    def _():
        to_down.wait_recv()

    for b in range(2):
        summed = (
            taps[0][b] * halo[0].astype(F32)
            + taps[1][b] * halo[1].astype(F32)
            + taps[2][b] * halo[2].astype(F32)
        ).astype(BF)
        blended = (mix(summed, b).astype(F32) + polar[b].astype(F32)).astype(BF)
        mixed_all[c, b * rows : (b + 1) * rows, :] = blended
    to_mix = remote(mixed_all.at[c], mixed_all.at[c], h_send.at[3], h_recv.at[3], sibling)
    to_mix.start()
    total = middle[...].astype(F32) + jnp.dot(own_coeffs, mixed_all[c], preferred_element_type=F32)
    to_mix.wait_recv()
    total = total + jnp.dot(side_coeffs, mixed_all[1 - c], preferred_element_type=F32)
    out[...] = total.astype(BF)

    gather_q.finish()
    gather_o.finish()
    for d in tok_copies + att_copies + [to_side, to_mix]:
        d.wait_send()

    @pl.when(inner_up)
    def _():
        to_up.wait_send()

    @pl.when(inner_down)
    def _():
        to_down.wait_send()


def fused_device(
    tokens, gain_attn, w_qkv, key_bias, w_out, gain_conv, w_conv, lat_taps, lon_half, lat_half, quad_off
):
    rows, width = tokens.shape[1:]
    shard = w_qkv.shape[0]
    heads = key_bias.shape[1]
    lat_count = width // shard
    nx = 2
    nz = lat_count // nx
    vmem = pl.BlockSpec(memory_space=pltpu.VMEM)
    smem = pl.BlockSpec(memory_space=pltpu.SMEM)
    dma = pltpu.SemaphoreType.DMA
    kinds = 2 * nz - 1
    out = pl.pallas_call(
        lambda *refs: fused_kernel(nx, nz, *refs),
        out_shape=jax.ShapeDtypeStruct((rows, width), BF),
        in_specs=[smem] * 4 + [vmem] * 7,
        out_specs=vmem,
        scratch_shapes=[
            pltpu.VMEM((width, 3 * width // 4), BF),
            pltpu.VMEM((width, width), BF),
            pltpu.VMEM((2, 2 * rows, width), BF),
            pltpu.VMEM((2, 2 * rows, width), BF),
            pltpu.VMEM((2, heads, rows), BF),
            pltpu.VMEM((heads, 2 * rows), F32),
            pltpu.VMEM((2, 2 * rows, width // 4), BF),
            pltpu.VMEM((4, rows, width // 4), BF),
            pltpu.VMEM((3, rows, width), BF),
            pltpu.VMEM((rows, width), BF),
            pltpu.VMEM((2, width, 128), BF),
            pltpu.VMEM((2, 2 * rows, width), BF),
            pltpu.VMEM((rows, width), BF),
            dma((kinds, 3)),
            dma((lat_count,)),
            dma((kinds, 3)),
            dma((lat_count,)),
            dma((kinds + nz,)),
            dma((lat_count,)),
            dma((4,)),
            dma((4,)),
            dma((3,)),
            dma((4,)),
            dma((4,)),
            dma((4,)),
        ],
        compiler_params=pltpu.CompilerParams(
            collective_id=0, has_side_effects=True, vmem_limit_bytes=48 * 1024 * 1024
        ),
    )(
        lat_taps, lon_half, lat_half, quad_off,
        tokens[0], gain_attn[None], w_qkv, key_bias[0], w_out, gain_conv[None], w_conv,
    )
    return out[None]


def solution(mesh):
    sizes = (mesh.shape["groups"], mesh.shape["lat"], mesh.shape["lon"])
    return jax.shard_map(
        fused_device if sizes == (2, 8, 2) else per_device,
        mesh=mesh,
        in_specs=(
            P(("groups", "lat"), "lon", None),
            P(),
            P("lat", None),
            P("lat", None, "lon"),
            P("lat", None),
            P(),
            P(),
            P(),
            P("lat"),
            P("lat"),
            P("lat"),
        ),
        out_specs=P(("groups", "lat"), "lon", None),
        check_vma=False,
    )
```

```python
import jax
import jax.numpy as jnp
from jax import lax
from jax.experimental import pallas as pl
from jax.experimental.pallas import tpu as pltpu
from jax.sharding import PartitionSpec as P


def padded(cells, sides, width):
    for axis, dim in sides:
        count = lax.axis_size(axis)
        ends = count - 1
        head = lax.slice_in_dim(cells, 0, width, axis=dim)
        tail = lax.slice_in_dim(cells, cells.shape[dim] - width, cells.shape[dim], axis=dim)
        cells = jnp.concatenate(
            [
                lax.ppermute(tail, axis, [(i, (i + 1) % count) for i in range(ends)]),
                cells,
                lax.ppermute(head, axis, [((i + 1) % count, i) for i in range(ends)]),
            ],
            axis=dim,
        )
    return cells


def layer_norm(inputs, gain):
    values = inputs.astype(jnp.float32)
    average = jnp.mean(values, axis=-1, keepdims=True)
    centered = values - average
    variance = jnp.mean(centered * centered, axis=-1, keepdims=True)
    return centered * lax.rsqrt(variance + 1e-05) * gain


def group_mix(inputs, w_conv):
    basis, length, channels = inputs.shape
    group_width = w_conv.shape[2]
    groups = channels // group_width
    mixed_rows = jnp.einsum(
        "kjgc,kgce->kjge",
        inputs.reshape(basis, length, groups, group_width),
        w_conv.reshape(basis, groups, group_width, group_width),
        preferred_element_type=jnp.float32,
    )
    return mixed_rows.reshape(basis, length, channels).astype(jnp.bfloat16)


def lon_weights(row_ids, col_ids, half_width, lon_total):
    offset_lon = (
        jnp.mod(col_ids[None, :] - row_ids[:, None] + lon_total // 2, lon_total) - lon_total // 2
    )
    distance = jnp.abs(offset_lon).astype(jnp.float32)
    span_plus = (half_width + 1).astype(jnp.float32)
    tent_weight = jnp.where(
        distance <= half_width.astype(jnp.float32), (1.0 - distance / span_plus) / span_plus, 0.0
    )
    odd_weight = tent_weight * offset_lon.astype(jnp.float32) / span_plus
    return jnp.stack([tent_weight, odd_weight]).astype(jnp.bfloat16)


def start_state(query_count, head_count, head_dim):
    running_max = jnp.full((head_count, query_count), -jnp.inf, jnp.float32)
    running_sum = jnp.zeros((head_count, query_count), jnp.float32)
    running_out = jnp.zeros((query_count, head_count, head_dim), jnp.float32)
    return (running_max, running_sum, running_out)


def attend_keys(carry_state, queries, key_rows, value_rows, bias_rows, score_scale):
    key_count = key_rows.shape[0]
    for offset in range(0, key_count, 128):
        running_max, running_sum, running_out = carry_state
        key_block = key_rows[offset : offset + 128]
        value_block = value_rows[offset : offset + 128]
        bias_block = bias_rows[offset : offset + 128]
        scores = (
            jnp.einsum("qhd,khd->hqk", queries, key_block, preferred_element_type=jnp.float32)
            * score_scale
        )
        scores = scores + bias_block.T.astype(jnp.float32)[:, None, :]
        new_max = jnp.maximum(running_max, jnp.max(scores, axis=-1))
        rescale = jnp.exp(running_max - new_max)
        exp_scores = jnp.exp(scores - new_max[:, :, None])
        running_sum = running_sum * rescale + jnp.sum(exp_scores, axis=-1)
        running_out = running_out * rescale.T[:, :, None] + jnp.einsum(
            "hqk,khd->qhd",
            exp_scores.astype(jnp.bfloat16),
            value_block,
            preferred_element_type=jnp.float32,
        )
        carry_state = (new_max, running_sum, running_out)
    return carry_state


def finish_state(carry_state):
    running_max, running_sum, running_out = carry_state
    finished = running_out / running_sum.T[:, :, None]
    return finished.reshape(finished.shape[0], -1).astype(jnp.bfloat16)


def lon_conv(blended, half_width, first_col, out_cols):
    lon_total = blended.shape[1]
    block_cols = min(128, lon_total)
    block_count = lon_total // block_cols
    first_block = jnp.floor_divide(first_col - half_width, block_cols)
    last_block = jnp.floor_divide(first_col + out_cols - 1 + half_width, block_cols)
    turn_count = jnp.minimum(block_count, last_block - first_block + 1)
    row_ids = first_col + jnp.arange(out_cols, dtype=jnp.int32)

    def add_block(turn_index, running_out):
        block_at = jnp.mod(first_block + turn_index, block_count)
        lon_block = lax.dynamic_slice_in_dim(blended, block_at * block_cols, block_cols, 1)
        col_ids = block_at * block_cols + jnp.arange(block_cols, dtype=jnp.int32)
        coeffs = lon_weights(row_ids, col_ids, half_width, lon_total)
        return running_out + jnp.einsum(
            "kjc,kcd->jd", coeffs, lon_block, preferred_element_type=jnp.float32
        )

    initial = jnp.zeros((out_cols, blended.shape[2]), jnp.float32)
    return lax.fori_loop(0, turn_count, add_block, initial)


def per_device(
    tokens,
    gain_attn,
    w_qkv,
    key_bias,
    w_out,
    gain_conv,
    w_conv,
    lat_taps,
    lon_half,
    lat_half,
    quad_off,
):
    own_tokens = tokens[0]
    count_lon, model_width = own_tokens.shape
    head_count = key_bias.shape[1]
    head_dim = model_width // head_count
    score_scale = head_dim ** (-0.5)
    lon_place = lax.axis_index("lon")
    normed = layer_norm(own_tokens, gain_attn).astype(jnp.bfloat16)
    bias_rows = key_bias[0].T
    full_qkv, full_out = (
        lax.all_gather(w_qkv, "lat", axis=0, tiled=True),
        lax.all_gather(w_out, "lat", axis=0, tiled=True),
    )
    projected = jnp.dot(normed, full_qkv, preferred_element_type=jnp.float32).astype(jnp.bfloat16)
    queries = projected[:, :model_width].reshape(count_lon, head_count, head_dim)
    key_here = projected[:, model_width : 2 * model_width]
    value_here = projected[:, 2 * model_width :]
    key_piece = lax.all_gather(key_here, "lon", axis=0, tiled=True)
    value_piece = lax.all_gather(value_here, "lon", axis=0, tiled=True)
    bias_piece = lax.all_gather(bias_rows, "lon", axis=0, tiled=True)
    length = key_piece.shape[0]
    carry_state = attend_keys(
        start_state(count_lon, head_count, head_dim),
        queries,
        key_piece.reshape(length, head_count, head_dim),
        value_piece.reshape(length, head_count, head_dim),
        bias_piece,
        score_scale,
    )
    attended = finish_state(carry_state)
    branch_out = jnp.dot(attended, full_out, preferred_element_type=jnp.float32)
    middle = (own_tokens.astype(jnp.float32) + branch_out).astype(jnp.bfloat16)
    conv_in = layer_norm(middle, gain_conv).astype(jnp.bfloat16)
    stacked = padded(conv_in[None], (("lat", 0),), 1)
    lat_row = lax.axis_index("lat")
    last_band = lax.axis_size("lat") - 1
    offsets = jnp.arange(3, dtype=jnp.int32) - 1
    one_hot = (
        (quad_off[0] + offsets + 1)[:, None]
        == jnp.arange(lat_taps.shape[0], dtype=jnp.int32)[None, :]
    ).astype(jnp.float32)
    tap_vals = jnp.dot(one_hot, lat_taps, precision=lax.Precision.HIGHEST)
    tap_vals = jnp.where((jnp.abs(offsets) <= lat_half[0])[:, None], tap_vals, 0.0)
    summed = jnp.einsum(
        "rk,rjd->kjd", tap_vals, stacked.astype(jnp.float32), precision=lax.Precision.HIGHEST
    ).astype(jnp.bfloat16)
    pole_gain = jnp.where(lat_row == 0, tap_vals[0], 0.0) + jnp.where(
        lat_row == last_band, tap_vals[2], 0.0
    )
    first_col = lon_place * count_lon
    pole_rows = (pole_gain[:, None, None] * conv_in.astype(jnp.float32)[None]).astype(jnp.bfloat16)
    mixed_rows = group_mix(summed, w_conv)
    pole_mixed = group_mix(pole_rows, w_conv)
    circle_rows, pole_all = (
        lax.all_gather(mixed_rows, "lon", axis=1, tiled=True),
        lax.all_gather(pole_mixed, "lon", axis=1, tiled=True),
    )
    lon_total = circle_rows.shape[1]
    blended = (
        circle_rows.astype(jnp.float32)
        + jnp.roll(pole_all, -(lon_total // 2), axis=1).astype(jnp.float32)
    ).astype(jnp.bfloat16)
    conv_out = lon_conv(blended, lon_half[0], first_col, count_lon)
    return (middle.astype(jnp.float32) + conv_out).astype(jnp.bfloat16)[None]


BF = jnp.bfloat16
F32 = jnp.float32
MESH = pl.DeviceIdType.MESH


def norm_rows(values, gain):
    values = values.astype(F32)
    average = jnp.mean(values, axis=-1, keepdims=True)
    centered = values - average
    variance = jnp.mean(centered * centered, axis=-1, keepdims=True)
    return (centered * lax.rsqrt(variance + 1e-05) * gain).astype(BF)


def fused_kernel(
    nx, nz,
    lat_taps_h, lon_half_h, lat_half_h, quad_off_h,
    tokens_h, gain_attn_h, w_qkv_h, key_bias_h, w_out_h, gain_conv_h, w_conv_h,
    out,
    lat_taps, lon_half, lat_half, quad_off, gain_attn, w_qkv, gain_conv, w_conv, load,
    wq, wo, tok, normed, bias, bias_f, att_out, att_in, halo, other_in, mixer, mixed_all, middle,
    q_send, q_recv, o_send, o_recv, r_send, r_recv, t_send, t_recv, a_send, a_recv, h_send, h_recv, n_send, n_recv, f_send, f_recv,
):
    y, place, c = lax.axis_index("groups"), lax.axis_index("lat"), lax.axis_index("lon")
    z, x = lax.div(place, nx), lax.rem(place, nx)
    quad = y * 2 + c
    x_peer = (y, z * nx + (1 - x), c)
    z_up, z_down = (y, place + nx, c), (y, place - nx, c)
    sibling = (y, place, 1 - c)
    y_peer = (1 - y, place, c)
    diagonal = (1 - y, place, 1 - c)
    has_up, has_down = z < nz - 1, z > 0
    lat_count = nx * nz
    shard = w_qkv.shape[0]
    width = tokens_h.shape[1]
    rows = tokens_h.shape[0]
    head = 64
    part = width // 4
    half = width // 2

    barrier = pltpu.get_barrier_semaphore()

    def greet(device):
        pl.semaphore_signal(barrier, inc=1, device_id=device, device_id_type=MESH)

    for device in (x_peer, sibling, y_peer, diagonal):
        greet(device)
    for cond, device in ((has_up, z_up), (has_down, z_down)):
        @pl.when(cond)
        def _(device=device):
            greet(device)

    own_tokens = tok.at[y, pl.ds(c * rows, rows), :]
    loads = [
        pltpu.make_async_copy(source, target, load.at[k])
        for k, (source, target) in enumerate(
            (
                (w_qkv_h, w_qkv),
                (tokens_h, own_tokens),
                (gain_attn_h, gain_attn),
                (w_conv_h, w_conv),
                (key_bias_h, bias.at[c]),
                (w_out_h, wo.at[pl.ds(place * shard, shard), :]),
                (gain_conv_h, gain_conv),
                (lat_taps_h, lat_taps),
                (lon_half_h, lon_half),
                (lat_half_h, lat_half),
                (quad_off_h, quad_off),
            )
        )
    ]
    for copy in loads:
        copy.start()
    loads[0].wait()

    for pick in range(4):
        @pl.when(quad == pick)
        def _(pick=pick):
            wq[pl.ds(place * shard, shard), :] = jnp.concatenate(
                [w_qkv[:, j * width + pick * part : j * width + (pick + 1) * part] for j in range(3)],
                axis=1,
            )
    loads[1].wait()

    pl.semaphore_wait(
        barrier,
        4 + has_up.astype(jnp.int32) + has_down.astype(jnp.int32),
    )

    def remote(source, target, send, recv, device):
        return pltpu.make_async_remote_copy(
            src_ref=source, dst_ref=target, send_sem=send, recv_sem=recv,
            device_id=device, device_id_type=MESH,
        )

    def q_at(slot, h):
        return wq.at[pl.ds(slot * shard + h * (shard // 2), shard // 2), :]

    def o_at(slot, h=0):
        return wo.at[pl.ds(slot * shard, shard), pl.ds(c * half, half)]

    def o_other(slot):
        return wo.at[pl.ds(slot * shard, shard), pl.ds((1 - c) * half, half)]

    class Gather:
        def __init__(self, at, send, recv, relay, chunks):
            self.at, self.send, self.recv, self.relay = at, send, recv, relay
            self.chunks = range(chunks)

        def copy(self, slot, k, way, device, h):
            return remote(
                self.at(slot, h), self.at(slot, h),
                self.send.at[k, way, h], self.recv.at[slot, h], device,
            )

        def hop(self, slot, k):
            return remote(self.at(slot), self.at(slot), r_send.at[k], r_recv.at[slot], sibling)

        def own(self, act):
            for h in self.chunks:
                @pl.when(has_up)
                def _(h=h):
                    act(self.copy(place, 0, 1, z_up, h))

                @pl.when(has_down)
                def _(h=h):
                    act(self.copy(place, 0, 2, z_down, h))

                act(self.copy(place, 0, 0, x_peer, h))

        def step(self, t, receive):
            act = (lambda d: d.start()) if receive else (lambda d: d.wait_send())
            for h in self.chunks:
                for sign, reach, onward, device, way, k in (
                    (-1, z >= t, has_up, z_up, 1, t),
                    (1, z + t <= nz - 1, has_down, z_down, 2, nz - 1 + t),
                ):
                    slot = (z + sign * t) * nx + x

                    @pl.when(reach)
                    def _(slot=slot, k=k, h=h):
                        if receive:
                            self.copy(slot, k, 0, x_peer, h).wait_recv()

                    @pl.when(jnp.logical_and(reach, onward))
                    def _(slot=slot, k=k, way=way, device=device, h=h):
                        act(self.copy(slot, k, way, device, h))

                    @pl.when(reach)
                    def _(slot=slot, k=k, h=h):
                        act(self.copy(slot, k, 0, x_peer, h))
                        if self.relay:
                            act(self.hop(slot, k))

        def across(self):
            for zz in range(nz):
                slot = zz * nx + (1 - x)
                for h in self.chunks:
                    self.copy(slot, 0, 0, x_peer, h).wait_recv()
                if self.relay:
                    self.hop(slot, 2 * nz - 1 + zz).start()

        def finish(self):
            self.own(lambda d: d.wait_send())
            for t in range(1, nz):
                self.step(t, False)
            if self.relay:
                for zz in range(nz):
                    slot = zz * nx + (1 - x)
                    self.hop(slot, 2 * nz - 1 + zz).wait_send()

    gather_q = Gather(q_at, q_send, q_recv, False, 2)
    gather_o = Gather(o_at, o_send, o_recv, True, 1)
    start = lambda d: d.start()

    gather_q.own(start)

    def tok_at(yy, cc):
        return tok.at[yy, pl.ds(cc * rows, rows), :]

    tok_copies = [
        remote(tok_at(y, c), tok_at(y, c), t_send.at[0], t_recv.at[0], y_peer),
        remote(tok_at(y, c), tok_at(y, c), t_send.at[1], t_recv.at[1], sibling),
        remote(tok_at(1 - y, c), tok_at(1 - y, c), t_send.at[2], t_recv.at[2], sibling),
        remote(bias.at[c], bias.at[c], t_send.at[3], t_recv.at[3], sibling),
    ]
    tok_copies[0].start()
    tok_copies[1].start()
    loads[4].wait()
    tok_copies[3].start()
    loads[2].wait()
    gain_a = gain_attn[...][None]

    def norm_block(yy, cc):
        normed[yy, pl.ds(cc * rows, rows), :] = norm_rows(tok[yy, pl.ds(cc * rows, rows), :], gain_a)

    norm_block(y, c)
    loads[3].wait()
    pair_row = lax.broadcasted_iota(jnp.int32, (2 * head, width), 0)
    pair_col = lax.broadcasted_iota(jnp.int32, (2 * head, width), 1)
    same = lax.rem(lax.div(pair_col, head), 2) == lax.div(pair_row, head)
    for b in range(2):
        wide = jnp.concatenate([w_conv[b], w_conv[b]], axis=0).astype(F32)
        mixer[b] = jnp.where(same, wide, 0.0).astype(BF)

    gather_q.step(1, True)
    tok_copies[1].wait_recv()
    norm_block(y, 1 - c)
    tok_copies[0].wait_recv()
    tok_copies[2].start()
    gather_q.step(2, True)
    norm_block(1 - y, c)
    loads[5].wait()
    gather_o.own(start)
    tok_copies[2].wait_recv()
    norm_block(1 - y, 1 - c)
    gather_q.step(3, True)
    tok_copies[3].wait_recv()
    bias_f[...] = jnp.concatenate([bias[0], bias[1]], axis=1).astype(F32)
    gather_q.across()
    gather_o.step(1, True)

    def att_copy(r, to_c, k, device):
        return remote(
            att_out.at[r, pl.ds(to_c * rows, rows), :], att_in.at[quad],
            a_send.at[k], a_recv.at[quad], device,
        )

    att_copies = [
        att_copy(0, c, 0, y_peer), att_copy(0, 1 - c, 1, diagonal), att_copy(1, 1 - c, 2, sibling)
    ]

    def attend(sample, r, between):
        projected = jnp.dot(normed[sample], wq[...], preferred_element_type=F32).astype(BF)
        between()
        pieces = []
        for h in range(3):
            queries = projected[:, h * head : (h + 1) * head] * jnp.asarray(head ** -0.5, BF)
            keys = projected[:, part + h * head : part + (h + 1) * head]
            vals = projected[:, 2 * part + h * head : 2 * part + (h + 1) * head]
            scores = lax.dot_general(
                queries, keys, (((1,), (1,)), ((), ())), preferred_element_type=F32
            ) + bias_f[pl.ds(quad * 3 + h, 1), :]
            expd = jnp.exp(scores - jnp.max(scores, axis=-1, keepdims=True))
            totals = jnp.sum(expd, axis=-1, keepdims=True)
            pieces.append(jnp.dot(expd.astype(BF), vals, preferred_element_type=F32) / totals)
        att_out[r] = jnp.concatenate(pieces, axis=1).astype(BF)

    attend(1 - y, 0, lambda: gather_o.step(2, True))
    att_copies[0].start()
    att_copies[1].start()
    gather_o.step(3, True)
    attend(y, 1, gather_o.across)
    att_copies[2].start()
    att_in[quad] = att_out[1, pl.ds(c * rows, rows), :]

    for t in range(1, nz):
        for sign, reach in ((-1, z >= t), (1, z + t <= nz - 1)):
            @pl.when(reach)
            def _(slot=(z + sign * t) * nx + x):
                remote(o_other(slot), o_other(slot), r_send.at[0], r_recv.at[slot], sibling).wait_recv()
    for zz in range(nz):
        slot = zz * nx + (1 - x)
        remote(o_other(slot), o_other(slot), r_send.at[0], r_recv.at[slot], sibling).wait_recv()
    for source in (y * 2 + (1 - c), (1 - y) * 2 + c, (1 - y) * 2 + (1 - c)):
        remote(att_in.at[source], att_in.at[source], a_send.at[0], a_recv.at[source], sibling).wait_recv()
    branch = tok[y, pl.ds(c * rows, rows), :].astype(F32)
    for p in range(4):
        branch = branch + jnp.dot(
            att_in[p], wo[p * part : (p + 1) * part, :], preferred_element_type=F32
        )
    mid = branch.astype(BF)
    middle[...] = mid
    for k in range(6, 11):
        loads[k].wait()
    conv_in = norm_rows(mid, gain_conv[...][None])
    halo[1] = conv_in

    near, far = 2 * (1 - x), 2 * x
    passes = jnp.logical_or(jnp.logical_and(x == 0, has_up), jnp.logical_and(x == 1, has_down))
    gets = jnp.logical_or(jnp.logical_and(x == 0, has_down), jnp.logical_and(x == 1, has_up))
    onward = (y, place + nx * (1 - 2 * x), c)
    pieces = 4
    piece = rows // pieces

    def halo_at(which, k):
        return halo.at[which, pl.ds(k * piece, piece), :]

    to_near = [
        remote(halo_at(1, k), halo_at(far, k), n_send.at[k], n_recv.at[k], x_peer)
        for k in range(pieces)
    ]
    from_near = [
        remote(halo_at(1, k), halo_at(near, k), n_send.at[k], n_recv.at[k], x_peer)
        for k in range(pieces)
    ]
    to_far = [
        remote(halo_at(near, k), halo_at(far, k), f_send.at[k], f_recv.at[k], onward)
        for k in range(pieces)
    ]
    for d in to_near:
        d.start()
    to_side = remote(halo.at[1], other_in, h_send.at[2], h_recv.at[2], sibling)
    to_side.start()

    @pl.when(jnp.logical_not(gets))
    def _():
        halo[far] = jnp.zeros((rows, width), BF)

    base = quad_off[0]
    reach_lat = lat_half[0]
    wide_ok = reach_lat >= 1
    taps = [
        [
            lat_taps[b, base + r] if r == 1 else jnp.where(wide_ok, lat_taps[b, base + r], 0.0)
            for b in range(2)
        ]
        for r in range(3)
    ]
    span = (lon_half[0] + 1).astype(F32)
    limit = lon_half[0].astype(F32)
    diff = lax.broadcasted_iota(jnp.int32, (rows, rows), 1) - lax.broadcasted_iota(
        jnp.int32, (rows, rows), 0
    )

    def coeffs(offset):
        offset = offset.astype(F32)
        distance = jnp.abs(offset)
        tent = jnp.where(distance <= limit, (1.0 - distance / span) / span, 0.0)
        odd = tent * offset / span
        return jnp.concatenate([tent.astype(BF), odd.astype(BF)], axis=1)

    own_coeffs = coeffs(diff)
    side_coeffs = coeffs(jnp.where(diff >= 0, diff - rows, diff + rows))

    def mix(values, b):
        return jnp.concatenate(
            [
                lax.dot_general(
                    values[:, p * 2 * head : (p + 1) * 2 * head],
                    mixer[b, :, p * 2 * head : (p + 1) * 2 * head],
                    (((1,), (1,)), ((), ())),
                    preferred_element_type=F32,
                )
                for p in range(width // (2 * head))
            ],
            axis=1,
        ).astype(BF)

    for k in range(pieces):
        from_near[k].wait_recv()

        @pl.when(passes)
        def _(k=k):
            to_far[k].start()

    to_side.wait_recv()
    side_rows = other_in[...].astype(F32)
    polar = []
    for b in range(2):
        gain = jnp.where(place == 0, taps[0][b], 0.0) + jnp.where(
            place == lat_count - 1, taps[2][b], 0.0
        )
        polar.append(mix((gain * side_rows).astype(BF), b))

    @pl.when(gets)
    def _():
        for d in to_far:
            d.wait_recv()

    for b in range(2):
        summed = (
            taps[0][b] * halo[0].astype(F32)
            + taps[1][b] * halo[1].astype(F32)
            + taps[2][b] * halo[2].astype(F32)
        ).astype(BF)
        blended = (mix(summed, b).astype(F32) + polar[b].astype(F32)).astype(BF)
        mixed_all[c, b * rows : (b + 1) * rows, :] = blended
    to_mix = remote(mixed_all.at[c], mixed_all.at[c], h_send.at[3], h_recv.at[3], sibling)
    to_mix.start()
    total = middle[...].astype(F32) + jnp.dot(own_coeffs, mixed_all[c], preferred_element_type=F32)
    to_mix.wait_recv()
    total = total + jnp.dot(side_coeffs, mixed_all[1 - c], preferred_element_type=F32)
    out[...] = total.astype(BF)

    gather_q.finish()
    gather_o.finish()
    for d in tok_copies + att_copies + [to_side, to_mix]:
        d.wait_send()

    for d in to_near:
        d.wait_send()

    @pl.when(passes)
    def _():
        for d in to_far:
            d.wait_send()


def fused_device(
    tokens, gain_attn, w_qkv, key_bias, w_out, gain_conv, w_conv, lat_taps, lon_half, lat_half, quad_off
):
    rows, width = tokens.shape[1:]
    shard = w_qkv.shape[0]
    heads = key_bias.shape[1]
    lat_count = width // shard
    nx = 2
    nz = lat_count // nx
    vmem = pl.BlockSpec(memory_space=pltpu.VMEM)
    anywhere = pl.BlockSpec(memory_space=pltpu.HBM)
    dma = pltpu.SemaphoreType.DMA
    kinds = 2 * nz - 1
    out = pl.pallas_call(
        lambda *refs: fused_kernel(nx, nz, *refs),
        out_shape=jax.ShapeDtypeStruct((rows, width), BF),
        in_specs=[anywhere] * 11,
        out_specs=vmem,
        scratch_shapes=[
            pltpu.SMEM((2, lat_taps.shape[0]), F32),
            pltpu.SMEM((1,), jnp.int32),
            pltpu.SMEM((1,), jnp.int32),
            pltpu.SMEM((1,), jnp.int32),
            pltpu.VMEM((width,), F32),
            pltpu.VMEM(w_qkv.shape, BF),
            pltpu.VMEM((width,), F32),
            pltpu.VMEM((2, 64, width), BF),
            dma((11,)),
            pltpu.VMEM((width, 3 * width // 4), BF),
            pltpu.VMEM((width, width), BF),
            pltpu.VMEM((2, 2 * rows, width), BF),
            pltpu.VMEM((2, 2 * rows, width), BF),
            pltpu.VMEM((2, heads, rows), BF),
            pltpu.VMEM((heads, 2 * rows), F32),
            pltpu.VMEM((2, 2 * rows, width // 4), BF),
            pltpu.VMEM((4, rows, width // 4), BF),
            pltpu.VMEM((3, rows, width), BF),
            pltpu.VMEM((rows, width), BF),
            pltpu.VMEM((2, 128, width), BF),
            pltpu.VMEM((2, 2 * rows, width), BF),
            pltpu.VMEM((rows, width), BF),
            dma((kinds, 3, 2)),
            dma((lat_count, 2)),
            dma((kinds, 3, 1)),
            dma((lat_count, 1)),
            dma((kinds + nz,)),
            dma((lat_count,)),
            dma((4,)),
            dma((4,)),
            dma((3,)),
            dma((4,)),
            dma((4,)),
            dma((4,)),
            dma((4,)),
            dma((4,)),
            dma((4,)),
            dma((4,)),
        ],
        compiler_params=pltpu.CompilerParams(
            collective_id=0, has_side_effects=True, vmem_limit_bytes=63 * 1024 * 1024
        ),
    )(
        lat_taps.T, lon_half, lat_half, quad_off,
        tokens[0], gain_attn, w_qkv, key_bias[0], w_out, gain_conv, jnp.swapaxes(w_conv, 1, 2),
    )
    return out[None]


def solution(mesh):
    sizes = (mesh.shape["groups"], mesh.shape["lat"], mesh.shape["lon"])
    return jax.shard_map(
        fused_device if sizes == (2, 8, 2) else per_device,
        mesh=mesh,
        in_specs=(
            P(("groups", "lat"), "lon", None),
            P(),
            P("lat", None),
            P("lat", None, "lon"),
            P("lat", None),
            P(),
            P(),
            P(),
            P("lat"),
            P("lat"),
            P("lat"),
        ),
        out_specs=P(("groups", "lat"), "lon", None),
        check_vma=False,
    )
```

```python
import jax
import jax.numpy as jnp
from jax import lax
from jax.experimental import pallas as pl
from jax.experimental.pallas import tpu as pltpu
from jax.sharding import PartitionSpec as P


def padded(cells, sides, width):
    for axis, dim in sides:
        count = lax.axis_size(axis)
        ends = count - 1
        head = lax.slice_in_dim(cells, 0, width, axis=dim)
        tail = lax.slice_in_dim(cells, cells.shape[dim] - width, cells.shape[dim], axis=dim)
        cells = jnp.concatenate(
            [
                lax.ppermute(tail, axis, [(i, (i + 1) % count) for i in range(ends)]),
                cells,
                lax.ppermute(head, axis, [((i + 1) % count, i) for i in range(ends)]),
            ],
            axis=dim,
        )
    return cells


def layer_norm(inputs, gain):
    values = inputs.astype(jnp.float32)
    average = jnp.mean(values, axis=-1, keepdims=True)
    centered = values - average
    variance = jnp.mean(centered * centered, axis=-1, keepdims=True)
    return centered * lax.rsqrt(variance + 1e-05) * gain


def group_mix(inputs, w_conv):
    basis, length, channels = inputs.shape
    group_width = w_conv.shape[2]
    groups = channels // group_width
    mixed_rows = jnp.einsum(
        "kjgc,kgce->kjge",
        inputs.reshape(basis, length, groups, group_width),
        w_conv.reshape(basis, groups, group_width, group_width),
        preferred_element_type=jnp.float32,
    )
    return mixed_rows.reshape(basis, length, channels).astype(jnp.bfloat16)


def lon_weights(row_ids, col_ids, half_width, lon_total):
    offset_lon = (
        jnp.mod(col_ids[None, :] - row_ids[:, None] + lon_total // 2, lon_total) - lon_total // 2
    )
    distance = jnp.abs(offset_lon).astype(jnp.float32)
    span_plus = (half_width + 1).astype(jnp.float32)
    tent_weight = jnp.where(
        distance <= half_width.astype(jnp.float32), (1.0 - distance / span_plus) / span_plus, 0.0
    )
    odd_weight = tent_weight * offset_lon.astype(jnp.float32) / span_plus
    return jnp.stack([tent_weight, odd_weight]).astype(jnp.bfloat16)


def start_state(query_count, head_count, head_dim):
    running_max = jnp.full((head_count, query_count), -jnp.inf, jnp.float32)
    running_sum = jnp.zeros((head_count, query_count), jnp.float32)
    running_out = jnp.zeros((query_count, head_count, head_dim), jnp.float32)
    return (running_max, running_sum, running_out)


def attend_keys(carry_state, queries, key_rows, value_rows, bias_rows, score_scale):
    key_count = key_rows.shape[0]
    for offset in range(0, key_count, 128):
        running_max, running_sum, running_out = carry_state
        key_block = key_rows[offset : offset + 128]
        value_block = value_rows[offset : offset + 128]
        bias_block = bias_rows[offset : offset + 128]
        scores = (
            jnp.einsum("qhd,khd->hqk", queries, key_block, preferred_element_type=jnp.float32)
            * score_scale
        )
        scores = scores + bias_block.T.astype(jnp.float32)[:, None, :]
        new_max = jnp.maximum(running_max, jnp.max(scores, axis=-1))
        rescale = jnp.exp(running_max - new_max)
        exp_scores = jnp.exp(scores - new_max[:, :, None])
        running_sum = running_sum * rescale + jnp.sum(exp_scores, axis=-1)
        running_out = running_out * rescale.T[:, :, None] + jnp.einsum(
            "hqk,khd->qhd",
            exp_scores.astype(jnp.bfloat16),
            value_block,
            preferred_element_type=jnp.float32,
        )
        carry_state = (new_max, running_sum, running_out)
    return carry_state


def finish_state(carry_state):
    running_max, running_sum, running_out = carry_state
    finished = running_out / running_sum.T[:, :, None]
    return finished.reshape(finished.shape[0], -1).astype(jnp.bfloat16)


def lon_conv(blended, half_width, first_col, out_cols):
    lon_total = blended.shape[1]
    block_cols = min(128, lon_total)
    block_count = lon_total // block_cols
    first_block = jnp.floor_divide(first_col - half_width, block_cols)
    last_block = jnp.floor_divide(first_col + out_cols - 1 + half_width, block_cols)
    turn_count = jnp.minimum(block_count, last_block - first_block + 1)
    row_ids = first_col + jnp.arange(out_cols, dtype=jnp.int32)

    def add_block(turn_index, running_out):
        block_at = jnp.mod(first_block + turn_index, block_count)
        lon_block = lax.dynamic_slice_in_dim(blended, block_at * block_cols, block_cols, 1)
        col_ids = block_at * block_cols + jnp.arange(block_cols, dtype=jnp.int32)
        coeffs = lon_weights(row_ids, col_ids, half_width, lon_total)
        return running_out + jnp.einsum(
            "kjc,kcd->jd", coeffs, lon_block, preferred_element_type=jnp.float32
        )

    initial = jnp.zeros((out_cols, blended.shape[2]), jnp.float32)
    return lax.fori_loop(0, turn_count, add_block, initial)


def per_device(
    tokens,
    gain_attn,
    w_qkv,
    key_bias,
    w_out,
    gain_conv,
    w_conv,
    lat_taps,
    lon_half,
    lat_half,
    quad_off,
):
    own_tokens = tokens[0]
    count_lon, model_width = own_tokens.shape
    head_count = key_bias.shape[1]
    head_dim = model_width // head_count
    score_scale = head_dim ** (-0.5)
    lon_place = lax.axis_index("lon")
    normed = layer_norm(own_tokens, gain_attn).astype(jnp.bfloat16)
    bias_rows = key_bias[0].T
    full_qkv, full_out = (
        lax.all_gather(w_qkv, "lat", axis=0, tiled=True),
        lax.all_gather(w_out, "lat", axis=0, tiled=True),
    )
    projected = jnp.dot(normed, full_qkv, preferred_element_type=jnp.float32).astype(jnp.bfloat16)
    queries = projected[:, :model_width].reshape(count_lon, head_count, head_dim)
    key_here = projected[:, model_width : 2 * model_width]
    value_here = projected[:, 2 * model_width :]
    key_piece = lax.all_gather(key_here, "lon", axis=0, tiled=True)
    value_piece = lax.all_gather(value_here, "lon", axis=0, tiled=True)
    bias_piece = lax.all_gather(bias_rows, "lon", axis=0, tiled=True)
    length = key_piece.shape[0]
    carry_state = attend_keys(
        start_state(count_lon, head_count, head_dim),
        queries,
        key_piece.reshape(length, head_count, head_dim),
        value_piece.reshape(length, head_count, head_dim),
        bias_piece,
        score_scale,
    )
    attended = finish_state(carry_state)
    branch_out = jnp.dot(attended, full_out, preferred_element_type=jnp.float32)
    middle = (own_tokens.astype(jnp.float32) + branch_out).astype(jnp.bfloat16)
    conv_in = layer_norm(middle, gain_conv).astype(jnp.bfloat16)
    stacked = padded(conv_in[None], (("lat", 0),), 1)
    lat_row = lax.axis_index("lat")
    last_band = lax.axis_size("lat") - 1
    offsets = jnp.arange(3, dtype=jnp.int32) - 1
    one_hot = (
        (quad_off[0] + offsets + 1)[:, None]
        == jnp.arange(lat_taps.shape[0], dtype=jnp.int32)[None, :]
    ).astype(jnp.float32)
    tap_vals = jnp.dot(one_hot, lat_taps, precision=lax.Precision.HIGHEST)
    tap_vals = jnp.where((jnp.abs(offsets) <= lat_half[0])[:, None], tap_vals, 0.0)
    summed = jnp.einsum(
        "rk,rjd->kjd", tap_vals, stacked.astype(jnp.float32), precision=lax.Precision.HIGHEST
    ).astype(jnp.bfloat16)
    pole_gain = jnp.where(lat_row == 0, tap_vals[0], 0.0) + jnp.where(
        lat_row == last_band, tap_vals[2], 0.0
    )
    first_col = lon_place * count_lon
    pole_rows = (pole_gain[:, None, None] * conv_in.astype(jnp.float32)[None]).astype(jnp.bfloat16)
    mixed_rows = group_mix(summed, w_conv)
    pole_mixed = group_mix(pole_rows, w_conv)
    circle_rows, pole_all = (
        lax.all_gather(mixed_rows, "lon", axis=1, tiled=True),
        lax.all_gather(pole_mixed, "lon", axis=1, tiled=True),
    )
    lon_total = circle_rows.shape[1]
    blended = (
        circle_rows.astype(jnp.float32)
        + jnp.roll(pole_all, -(lon_total // 2), axis=1).astype(jnp.float32)
    ).astype(jnp.bfloat16)
    conv_out = lon_conv(blended, lon_half[0], first_col, count_lon)
    return (middle.astype(jnp.float32) + conv_out).astype(jnp.bfloat16)[None]


BF = jnp.bfloat16
F32 = jnp.float32
MESH = pl.DeviceIdType.MESH


def norm_rows(values, gain):
    values = values.astype(F32)
    average = jnp.mean(values, axis=-1, keepdims=True)
    centered = values - average
    variance = jnp.mean(centered * centered, axis=-1, keepdims=True)
    return (centered * lax.rsqrt(variance + 1e-05) * gain).astype(BF)


def fused_kernel(
    nx, nz,
    lat_taps_h, lon_half_h, lat_half_h, quad_off_h,
    tokens_h, gain_attn_h, w_qkv_h, key_bias_h, w_out_h, gain_conv_h, w_conv_h,
    out,
    lat_taps, lon_half, lat_half, quad_off, gain_attn, w_qkv, gain_conv, w_conv, load,
    wq, wo, tok, normed, bias, bias_f, att_out, att_in, halo, other_in, mixer, mixed_all, middle,
    q_send, q_recv, o_send, o_recv, r_send, r_recv, t_send, t_recv, a_send, a_recv, h_send, h_recv, n_send, n_recv, f_send, f_recv,
    y_send, y_recv, g_send, g_recv,
):
    y, place, c = lax.axis_index("groups"), lax.axis_index("lat"), lax.axis_index("lon")
    z, x = lax.div(place, nx), lax.rem(place, nx)
    quad = y * 2 + c
    x_peer = (y, z * nx + (1 - x), c)
    z_up, z_down = (y, place + nx, c), (y, place - nx, c)
    sibling = (y, place, 1 - c)
    y_peer = (1 - y, place, c)
    diagonal = (1 - y, place, 1 - c)
    has_up, has_down = z < nz - 1, z > 0
    lat_count = nx * nz
    shard = w_qkv.shape[0]
    width = tokens_h.shape[1]
    rows = tokens_h.shape[0]
    head = 64
    part = width // 4
    half = width // 2

    barrier = pltpu.get_barrier_semaphore()

    def greet(device):
        pl.semaphore_signal(barrier, inc=1, device_id=device, device_id_type=MESH)

    for device in (x_peer, sibling, y_peer, diagonal):
        greet(device)
    for cond, device in ((has_up, z_up), (has_down, z_down)):
        @pl.when(cond)
        def _(device=device):
            greet(device)

    own_tokens = tok.at[y, pl.ds(c * rows, rows), :]
    loads = [
        pltpu.make_async_copy(source, target, load.at[k])
        for k, (source, target) in enumerate(
            (
                (w_qkv_h, w_qkv),
                (tokens_h, own_tokens),
                (gain_attn_h, gain_attn),
                (w_conv_h, w_conv),
                (key_bias_h, bias.at[c]),
                (w_out_h, wo.at[pl.ds(place * shard, shard), :]),
                (gain_conv_h, gain_conv),
                (lat_taps_h, lat_taps),
                (lon_half_h, lon_half),
                (lat_half_h, lat_half),
                (quad_off_h, quad_off),
            )
        )
    ]
    for copy in loads:
        copy.start()
    loads[0].wait()

    for pick in range(4):
        @pl.when(quad == pick)
        def _(pick=pick):
            wq[pl.ds(place * shard, shard), :] = jnp.concatenate(
                [w_qkv[:, j * width + pick * part : j * width + (pick + 1) * part] for j in range(3)],
                axis=1,
            )
    loads[1].wait()

    pl.semaphore_wait(
        barrier,
        4 + has_up.astype(jnp.int32) + has_down.astype(jnp.int32),
    )

    def remote(source, target, send, recv, device):
        return pltpu.make_async_remote_copy(
            src_ref=source, dst_ref=target, send_sem=send, recv_sem=recv,
            device_id=device, device_id_type=MESH,
        )

    def q_at(slot, h):
        return wq.at[pl.ds(slot * shard + h * (shard // 2), shard // 2), :]

    def o_at(slot, yy, cc):
        return wo.at[
            pl.ds(slot * shard + yy * (shard // 2), shard // 2), pl.ds(cc * half, half)
        ]

    class Gather:
        def __init__(self, at, send, recv, chunks):
            self.at, self.send, self.recv = at, send, recv
            self.chunks = range(chunks)

        def copy(self, slot, k, way, device, h):
            return remote(
                self.at(slot, h), self.at(slot, h),
                self.send.at[k, way, h], self.recv.at[slot, h], device,
            )

        def own(self, act):
            for h in self.chunks:
                @pl.when(has_up)
                def _(h=h):
                    act(self.copy(place, 0, 1, z_up, h))

                @pl.when(has_down)
                def _(h=h):
                    act(self.copy(place, 0, 2, z_down, h))

                act(self.copy(place, 0, 0, x_peer, h))

        def step(self, t, receive):
            act = (lambda d: d.start()) if receive else (lambda d: d.wait_send())
            for h in self.chunks:
                for sign, reach, onward, device, way, k in (
                    (-1, z >= t, has_up, z_up, 1, t),
                    (1, z + t <= nz - 1, has_down, z_down, 2, nz - 1 + t),
                ):
                    slot = (z + sign * t) * nx + x

                    @pl.when(reach)
                    def _(slot=slot, k=k, h=h):
                        if receive:
                            self.copy(slot, k, 0, x_peer, h).wait_recv()

                    @pl.when(jnp.logical_and(reach, onward))
                    def _(slot=slot, k=k, way=way, device=device, h=h):
                        act(self.copy(slot, k, way, device, h))

                    @pl.when(reach)
                    def _(slot=slot, k=k, h=h):
                        act(self.copy(slot, k, 0, x_peer, h))

        def across(self):
            for zz in range(nz):
                slot = zz * nx + (1 - x)
                for h in self.chunks:
                    self.copy(slot, 0, 0, x_peer, h).wait_recv()

        def finish(self):
            self.own(lambda d: d.wait_send())
            for t in range(1, nz):
                self.step(t, False)

    others = [(None, z * nx + (1 - x), ((has_up, 1, z_up), (has_down, 2, z_down)))]
    for t in range(1, nz):
        for sign, reach, going, way, device in (
            (-1, z >= t, has_up, 1, z_up), (1, z + t <= nz - 1, has_down, 2, z_down)
        ):
            for xx in range(nx):
                others.append(
                    (
                        reach,
                        (z + sign * t) * nx + xx,
                        ((jnp.logical_and(reach, going), way, device),),
                    )
                )

    def when(cond, run):
        if cond is None:
            run()
        else:
            pl.when(cond)(run)

    def o_copy(slot, k, way, device):
        return remote(
            o_at(slot, y, c), o_at(slot, y, c), o_send.at[k, way], o_recv.at[slot], device
        )

    def o_side(slot, k):
        return remote(o_at(slot, y, c), o_at(slot, y, c), r_send.at[k], r_recv.at[slot], sibling)

    def o_cross(slot, k):
        return remote(o_at(slot, y, c), o_at(slot, y, c), y_send.at[k], y_recv.at[slot], y_peer)

    def o_last(slot, k):
        return remote(
            o_at(slot, 1 - y, c), o_at(slot, 1 - y, c), g_send.at[k], g_recv.at[slot], sibling
        )

    def o_own(act):
        for cond, way, device in ((None, 0, x_peer), (has_up, 1, z_up), (has_down, 2, z_down)):
            when(cond, lambda way=way, device=device: act(o_copy(place, 13, way, device)))

    def o_forward(k, act):
        reach, slot, targets = others[k]
        for cond, way, device in targets:
            when(cond, lambda way=way, device=device: act(o_copy(slot, k, way, device)))

        def hand():
            act(o_cross(slot, k))
            act(o_side(slot, k))

        when(reach, hand)

    def o_step(ks):
        for k in ks:
            reach, slot, _ = others[k]
            when(reach, lambda slot=slot: o_copy(slot, 0, 0, x_peer).wait_recv())
            o_forward(k, lambda d: d.start())

    def o_collect():
        for k, (reach, slot, _) in enumerate(others):
            def run(slot=slot, k=k):
                o_cross(slot, k).wait_recv()
                o_last(slot, k).start()

            when(reach, run)
        for k, (reach, slot, _) in enumerate(others):
            def run(slot=slot, k=k):
                o_side(slot, k).wait_recv()
                o_last(slot, k).wait_recv()

            when(reach, run)

    def o_finish():
        o_own(lambda d: d.wait_send())
        for k, (reach, slot, _) in enumerate(others):
            o_forward(k, lambda d: d.wait_send())
            when(reach, lambda slot=slot, k=k: o_last(slot, k).wait_send())

    gather_q = Gather(q_at, q_send, q_recv, 2)
    start = lambda d: d.start()

    gather_q.own(start)

    def tok_at(yy, cc):
        return tok.at[yy, pl.ds(cc * rows, rows), :]

    tok_copies = [
        remote(tok_at(y, c), tok_at(y, c), t_send.at[0], t_recv.at[0], y_peer),
        remote(tok_at(y, c), tok_at(y, c), t_send.at[1], t_recv.at[1], sibling),
        remote(tok_at(1 - y, c), tok_at(1 - y, c), t_send.at[2], t_recv.at[2], sibling),
        remote(bias.at[c], bias.at[c], t_send.at[3], t_recv.at[3], sibling),
    ]
    tok_copies[0].start()
    tok_copies[1].start()
    loads[4].wait()
    tok_copies[3].start()
    loads[2].wait()
    gain_a = gain_attn[...][None]

    def norm_block(yy, cc):
        normed[yy, pl.ds(cc * rows, rows), :] = norm_rows(tok[yy, pl.ds(cc * rows, rows), :], gain_a)

    norm_block(y, c)
    loads[3].wait()
    pair_row = lax.broadcasted_iota(jnp.int32, (2 * head, width), 0)
    pair_col = lax.broadcasted_iota(jnp.int32, (2 * head, width), 1)
    same = lax.rem(lax.div(pair_col, head), 2) == lax.div(pair_row, head)
    for b in range(2):
        wide = jnp.concatenate([w_conv[b], w_conv[b]], axis=0).astype(F32)
        mixer[b] = jnp.where(same, wide, 0.0).astype(BF)

    gather_q.step(1, True)
    tok_copies[1].wait_recv()
    norm_block(y, 1 - c)
    tok_copies[0].wait_recv()
    tok_copies[2].start()
    gather_q.step(2, True)
    norm_block(1 - y, c)
    loads[5].wait()
    o_own(start)
    tok_copies[2].wait_recv()
    norm_block(1 - y, 1 - c)
    gather_q.step(3, True)
    o_step([0])
    tok_copies[3].wait_recv()
    bias_f[...] = jnp.concatenate([bias[0], bias[1]], axis=1).astype(F32)
    gather_q.across()
    o_step(range(1, 5))

    def att_copy(r, to_c, k, device):
        return remote(
            att_out.at[r, pl.ds(to_c * rows, rows), :], att_in.at[quad],
            a_send.at[k], a_recv.at[quad], device,
        )

    att_copies = [
        att_copy(0, c, 0, y_peer), att_copy(0, 1 - c, 1, diagonal), att_copy(1, 1 - c, 2, sibling)
    ]

    def attend(sample, r, between):
        projected = jnp.dot(normed[sample], wq[...], preferred_element_type=F32).astype(BF)
        between()
        pieces = []
        for h in range(3):
            queries = projected[:, h * head : (h + 1) * head] * jnp.asarray(head ** -0.5, BF)
            keys = projected[:, part + h * head : part + (h + 1) * head]
            vals = projected[:, 2 * part + h * head : 2 * part + (h + 1) * head]
            scores = lax.dot_general(
                queries, keys, (((1,), (1,)), ((), ())), preferred_element_type=F32
            ) + bias_f[pl.ds(quad * 3 + h, 1), :]
            expd = jnp.exp(scores - jnp.max(scores, axis=-1, keepdims=True))
            totals = jnp.sum(expd, axis=-1, keepdims=True)
            pieces.append(jnp.dot(expd.astype(BF), vals, preferred_element_type=F32) / totals)
        att_out[r] = jnp.concatenate(pieces, axis=1).astype(BF)

    attend(1 - y, 0, lambda: None)
    att_copies[0].start()
    att_copies[1].start()
    o_step(range(5, 9))
    attend(y, 1, lambda: None)
    att_copies[2].start()
    o_step(range(9, 13))
    att_in[quad] = att_out[1, pl.ds(c * rows, rows), :]

    o_collect()
    for source in (y * 2 + (1 - c), (1 - y) * 2 + c, (1 - y) * 2 + (1 - c)):
        remote(att_in.at[source], att_in.at[source], a_send.at[0], a_recv.at[source], sibling).wait_recv()
    branch = tok[y, pl.ds(c * rows, rows), :].astype(F32)
    for p in range(4):
        branch = branch + jnp.dot(
            att_in[p], wo[p * part : (p + 1) * part, :], preferred_element_type=F32
        )
    mid = branch.astype(BF)
    middle[...] = mid
    for k in range(6, 11):
        loads[k].wait()
    conv_in = norm_rows(mid, gain_conv[...][None])
    halo[1] = conv_in

    near, far = 2 * (1 - x), 2 * x
    passes = jnp.logical_or(jnp.logical_and(x == 0, has_up), jnp.logical_and(x == 1, has_down))
    gets = jnp.logical_or(jnp.logical_and(x == 0, has_down), jnp.logical_and(x == 1, has_up))
    onward = (y, place + nx * (1 - 2 * x), c)
    pieces = 4
    piece = rows // pieces

    def halo_at(which, k):
        return halo.at[which, pl.ds(k * piece, piece), :]

    to_near = [
        remote(halo_at(1, k), halo_at(far, k), n_send.at[k], n_recv.at[k], x_peer)
        for k in range(pieces)
    ]
    from_near = [
        remote(halo_at(1, k), halo_at(near, k), n_send.at[k], n_recv.at[k], x_peer)
        for k in range(pieces)
    ]
    to_far = [
        remote(halo_at(near, k), halo_at(far, k), f_send.at[k], f_recv.at[k], onward)
        for k in range(pieces)
    ]
    for d in to_near:
        d.start()
    to_side = remote(halo.at[1], other_in, h_send.at[2], h_recv.at[2], sibling)
    to_side.start()

    @pl.when(jnp.logical_not(gets))
    def _():
        halo[far] = jnp.zeros((rows, width), BF)

    base = quad_off[0]
    reach_lat = lat_half[0]
    wide_ok = reach_lat >= 1
    taps = [
        [
            lat_taps[b, base + r] if r == 1 else jnp.where(wide_ok, lat_taps[b, base + r], 0.0)
            for b in range(2)
        ]
        for r in range(3)
    ]
    span = (lon_half[0] + 1).astype(F32)
    limit = lon_half[0].astype(F32)
    diff = lax.broadcasted_iota(jnp.int32, (rows, rows), 1) - lax.broadcasted_iota(
        jnp.int32, (rows, rows), 0
    )

    def coeffs(offset):
        offset = offset.astype(F32)
        distance = jnp.abs(offset)
        tent = jnp.where(distance <= limit, (1.0 - distance / span) / span, 0.0)
        odd = tent * offset / span
        return jnp.concatenate([tent.astype(BF), odd.astype(BF)], axis=1)

    own_coeffs = coeffs(diff)
    side_coeffs = coeffs(jnp.where(diff >= 0, diff - rows, diff + rows))

    def mix(values, b):
        return jnp.concatenate(
            [
                lax.dot_general(
                    values[:, p * 2 * head : (p + 1) * 2 * head],
                    mixer[b, :, p * 2 * head : (p + 1) * 2 * head],
                    (((1,), (1,)), ((), ())),
                    preferred_element_type=F32,
                )
                for p in range(width // (2 * head))
            ],
            axis=1,
        ).astype(BF)

    for k in range(pieces):
        from_near[k].wait_recv()

        @pl.when(passes)
        def _(k=k):
            to_far[k].start()

    to_side.wait_recv()
    side_rows = other_in[...].astype(F32)
    polar = []
    for b in range(2):
        gain = jnp.where(place == 0, taps[0][b], 0.0) + jnp.where(
            place == lat_count - 1, taps[2][b], 0.0
        )
        polar.append(mix((gain * side_rows).astype(BF), b))

    @pl.when(gets)
    def _():
        for d in to_far:
            d.wait_recv()

    for b in range(2):
        summed = (
            taps[0][b] * halo[0].astype(F32)
            + taps[1][b] * halo[1].astype(F32)
            + taps[2][b] * halo[2].astype(F32)
        ).astype(BF)
        blended = (mix(summed, b).astype(F32) + polar[b].astype(F32)).astype(BF)
        mixed_all[c, b * rows : (b + 1) * rows, :] = blended
    to_mix = remote(mixed_all.at[c], mixed_all.at[c], h_send.at[3], h_recv.at[3], sibling)
    to_mix.start()
    total = middle[...].astype(F32) + jnp.dot(own_coeffs, mixed_all[c], preferred_element_type=F32)
    to_mix.wait_recv()
    total = total + jnp.dot(side_coeffs, mixed_all[1 - c], preferred_element_type=F32)
    out[...] = total.astype(BF)

    gather_q.finish()
    o_finish()
    for d in tok_copies + att_copies + [to_side, to_mix]:
        d.wait_send()

    for d in to_near:
        d.wait_send()

    @pl.when(passes)
    def _():
        for d in to_far:
            d.wait_send()


def fused_device(
    tokens, gain_attn, w_qkv, key_bias, w_out, gain_conv, w_conv, lat_taps, lon_half, lat_half, quad_off
):
    rows, width = tokens.shape[1:]
    shard = w_qkv.shape[0]
    heads = key_bias.shape[1]
    lat_count = width // shard
    nx = 2
    nz = lat_count // nx
    vmem = pl.BlockSpec(memory_space=pltpu.VMEM)
    anywhere = pl.BlockSpec(memory_space=pltpu.HBM)
    dma = pltpu.SemaphoreType.DMA
    kinds = 2 * nz - 1
    out = pl.pallas_call(
        lambda *refs: fused_kernel(nx, nz, *refs),
        out_shape=jax.ShapeDtypeStruct((rows, width), BF),
        in_specs=[anywhere] * 11,
        out_specs=vmem,
        scratch_shapes=[
            pltpu.SMEM((2, lat_taps.shape[0]), F32),
            pltpu.SMEM((1,), jnp.int32),
            pltpu.SMEM((1,), jnp.int32),
            pltpu.SMEM((1,), jnp.int32),
            pltpu.VMEM((width,), F32),
            pltpu.VMEM(w_qkv.shape, BF),
            pltpu.VMEM((width,), F32),
            pltpu.VMEM((2, 64, width), BF),
            dma((11,)),
            pltpu.VMEM((width, 3 * width // 4), BF),
            pltpu.VMEM((width, width), BF),
            pltpu.VMEM((2, 2 * rows, width), BF),
            pltpu.VMEM((2, 2 * rows, width), BF),
            pltpu.VMEM((2, heads, rows), BF),
            pltpu.VMEM((heads, 2 * rows), F32),
            pltpu.VMEM((2, 2 * rows, width // 4), BF),
            pltpu.VMEM((4, rows, width // 4), BF),
            pltpu.VMEM((3, rows, width), BF),
            pltpu.VMEM((rows, width), BF),
            pltpu.VMEM((2, 128, width), BF),
            pltpu.VMEM((2, 2 * rows, width), BF),
            pltpu.VMEM((rows, width), BF),
            dma((kinds, 3, 2)),
            dma((lat_count, 2)),
            dma((14, 3)),
            dma((lat_count,)),
            dma((13,)),
            dma((lat_count,)),
            dma((4,)),
            dma((4,)),
            dma((3,)),
            dma((4,)),
            dma((4,)),
            dma((4,)),
            dma((4,)),
            dma((4,)),
            dma((4,)),
            dma((4,)),
            dma((13,)),
            dma((lat_count,)),
            dma((13,)),
            dma((lat_count,)),
        ],
        compiler_params=pltpu.CompilerParams(
            collective_id=0, has_side_effects=True, vmem_limit_bytes=63 * 1024 * 1024
        ),
    )(
        lat_taps.T, lon_half, lat_half, quad_off,
        tokens[0], gain_attn, w_qkv, key_bias[0], w_out, gain_conv, jnp.swapaxes(w_conv, 1, 2),
    )
    return out[None]


def solution(mesh):
    sizes = (mesh.shape["groups"], mesh.shape["lat"], mesh.shape["lon"])
    return jax.shard_map(
        fused_device if sizes == (2, 8, 2) else per_device,
        mesh=mesh,
        in_specs=(
            P(("groups", "lat"), "lon", None),
            P(),
            P("lat", None),
            P("lat", None, "lon"),
            P("lat", None),
            P(),
            P(),
            P(),
            P("lat"),
            P("lat"),
            P("lat"),
        ),
        out_specs=P(("groups", "lat"), "lon", None),
        check_vma=False,
    )
```

```python
import jax
import jax.numpy as jnp
from jax import lax
from jax.experimental import pallas as pl
from jax.experimental.pallas import tpu as pltpu
from jax.sharding import PartitionSpec as P


def padded(cells, sides, width):
    for axis, dim in sides:
        count = lax.axis_size(axis)
        ends = count - 1
        head = lax.slice_in_dim(cells, 0, width, axis=dim)
        tail = lax.slice_in_dim(cells, cells.shape[dim] - width, cells.shape[dim], axis=dim)
        cells = jnp.concatenate(
            [
                lax.ppermute(tail, axis, [(i, (i + 1) % count) for i in range(ends)]),
                cells,
                lax.ppermute(head, axis, [((i + 1) % count, i) for i in range(ends)]),
            ],
            axis=dim,
        )
    return cells


def layer_norm(inputs, gain):
    values = inputs.astype(jnp.float32)
    average = jnp.mean(values, axis=-1, keepdims=True)
    centered = values - average
    variance = jnp.mean(centered * centered, axis=-1, keepdims=True)
    return centered * lax.rsqrt(variance + 1e-05) * gain


def group_mix(inputs, w_conv):
    basis, length, channels = inputs.shape
    group_width = w_conv.shape[2]
    groups = channels // group_width
    mixed_rows = jnp.einsum(
        "kjgc,kgce->kjge",
        inputs.reshape(basis, length, groups, group_width),
        w_conv.reshape(basis, groups, group_width, group_width),
        preferred_element_type=jnp.float32,
    )
    return mixed_rows.reshape(basis, length, channels).astype(jnp.bfloat16)


def lon_weights(row_ids, col_ids, half_width, lon_total):
    offset_lon = (
        jnp.mod(col_ids[None, :] - row_ids[:, None] + lon_total // 2, lon_total) - lon_total // 2
    )
    distance = jnp.abs(offset_lon).astype(jnp.float32)
    span_plus = (half_width + 1).astype(jnp.float32)
    tent_weight = jnp.where(
        distance <= half_width.astype(jnp.float32), (1.0 - distance / span_plus) / span_plus, 0.0
    )
    odd_weight = tent_weight * offset_lon.astype(jnp.float32) / span_plus
    return jnp.stack([tent_weight, odd_weight]).astype(jnp.bfloat16)


def start_state(query_count, head_count, head_dim):
    running_max = jnp.full((head_count, query_count), -jnp.inf, jnp.float32)
    running_sum = jnp.zeros((head_count, query_count), jnp.float32)
    running_out = jnp.zeros((query_count, head_count, head_dim), jnp.float32)
    return (running_max, running_sum, running_out)


def attend_keys(carry_state, queries, key_rows, value_rows, bias_rows, score_scale):
    key_count = key_rows.shape[0]
    for offset in range(0, key_count, 128):
        running_max, running_sum, running_out = carry_state
        key_block = key_rows[offset : offset + 128]
        value_block = value_rows[offset : offset + 128]
        bias_block = bias_rows[offset : offset + 128]
        scores = (
            jnp.einsum("qhd,khd->hqk", queries, key_block, preferred_element_type=jnp.float32)
            * score_scale
        )
        scores = scores + bias_block.T.astype(jnp.float32)[:, None, :]
        new_max = jnp.maximum(running_max, jnp.max(scores, axis=-1))
        rescale = jnp.exp(running_max - new_max)
        exp_scores = jnp.exp(scores - new_max[:, :, None])
        running_sum = running_sum * rescale + jnp.sum(exp_scores, axis=-1)
        running_out = running_out * rescale.T[:, :, None] + jnp.einsum(
            "hqk,khd->qhd",
            exp_scores.astype(jnp.bfloat16),
            value_block,
            preferred_element_type=jnp.float32,
        )
        carry_state = (new_max, running_sum, running_out)
    return carry_state


def finish_state(carry_state):
    running_max, running_sum, running_out = carry_state
    finished = running_out / running_sum.T[:, :, None]
    return finished.reshape(finished.shape[0], -1).astype(jnp.bfloat16)


def lon_conv(blended, half_width, first_col, out_cols):
    lon_total = blended.shape[1]
    block_cols = min(128, lon_total)
    block_count = lon_total // block_cols
    first_block = jnp.floor_divide(first_col - half_width, block_cols)
    last_block = jnp.floor_divide(first_col + out_cols - 1 + half_width, block_cols)
    turn_count = jnp.minimum(block_count, last_block - first_block + 1)
    row_ids = first_col + jnp.arange(out_cols, dtype=jnp.int32)

    def add_block(turn_index, running_out):
        block_at = jnp.mod(first_block + turn_index, block_count)
        lon_block = lax.dynamic_slice_in_dim(blended, block_at * block_cols, block_cols, 1)
        col_ids = block_at * block_cols + jnp.arange(block_cols, dtype=jnp.int32)
        coeffs = lon_weights(row_ids, col_ids, half_width, lon_total)
        return running_out + jnp.einsum(
            "kjc,kcd->jd", coeffs, lon_block, preferred_element_type=jnp.float32
        )

    initial = jnp.zeros((out_cols, blended.shape[2]), jnp.float32)
    return lax.fori_loop(0, turn_count, add_block, initial)


def per_device(
    tokens,
    gain_attn,
    w_qkv,
    key_bias,
    w_out,
    gain_conv,
    w_conv,
    lat_taps,
    lon_half,
    lat_half,
    quad_off,
):
    own_tokens = tokens[0]
    count_lon, model_width = own_tokens.shape
    head_count = key_bias.shape[1]
    head_dim = model_width // head_count
    score_scale = head_dim ** (-0.5)
    lon_place = lax.axis_index("lon")
    normed = layer_norm(own_tokens, gain_attn).astype(jnp.bfloat16)
    bias_rows = key_bias[0].T
    full_qkv, full_out = (
        lax.all_gather(w_qkv, "lat", axis=0, tiled=True),
        lax.all_gather(w_out, "lat", axis=0, tiled=True),
    )
    projected = jnp.dot(normed, full_qkv, preferred_element_type=jnp.float32).astype(jnp.bfloat16)
    queries = projected[:, :model_width].reshape(count_lon, head_count, head_dim)
    key_here = projected[:, model_width : 2 * model_width]
    value_here = projected[:, 2 * model_width :]
    key_piece = lax.all_gather(key_here, "lon", axis=0, tiled=True)
    value_piece = lax.all_gather(value_here, "lon", axis=0, tiled=True)
    bias_piece = lax.all_gather(bias_rows, "lon", axis=0, tiled=True)
    length = key_piece.shape[0]
    carry_state = attend_keys(
        start_state(count_lon, head_count, head_dim),
        queries,
        key_piece.reshape(length, head_count, head_dim),
        value_piece.reshape(length, head_count, head_dim),
        bias_piece,
        score_scale,
    )
    attended = finish_state(carry_state)
    branch_out = jnp.dot(attended, full_out, preferred_element_type=jnp.float32)
    middle = (own_tokens.astype(jnp.float32) + branch_out).astype(jnp.bfloat16)
    conv_in = layer_norm(middle, gain_conv).astype(jnp.bfloat16)
    stacked = padded(conv_in[None], (("lat", 0),), 1)
    lat_row = lax.axis_index("lat")
    last_band = lax.axis_size("lat") - 1
    offsets = jnp.arange(3, dtype=jnp.int32) - 1
    one_hot = (
        (quad_off[0] + offsets + 1)[:, None]
        == jnp.arange(lat_taps.shape[0], dtype=jnp.int32)[None, :]
    ).astype(jnp.float32)
    tap_vals = jnp.dot(one_hot, lat_taps, precision=lax.Precision.HIGHEST)
    tap_vals = jnp.where((jnp.abs(offsets) <= lat_half[0])[:, None], tap_vals, 0.0)
    summed = jnp.einsum(
        "rk,rjd->kjd", tap_vals, stacked.astype(jnp.float32), precision=lax.Precision.HIGHEST
    ).astype(jnp.bfloat16)
    pole_gain = jnp.where(lat_row == 0, tap_vals[0], 0.0) + jnp.where(
        lat_row == last_band, tap_vals[2], 0.0
    )
    first_col = lon_place * count_lon
    pole_rows = (pole_gain[:, None, None] * conv_in.astype(jnp.float32)[None]).astype(jnp.bfloat16)
    mixed_rows = group_mix(summed, w_conv)
    pole_mixed = group_mix(pole_rows, w_conv)
    circle_rows, pole_all = (
        lax.all_gather(mixed_rows, "lon", axis=1, tiled=True),
        lax.all_gather(pole_mixed, "lon", axis=1, tiled=True),
    )
    lon_total = circle_rows.shape[1]
    blended = (
        circle_rows.astype(jnp.float32)
        + jnp.roll(pole_all, -(lon_total // 2), axis=1).astype(jnp.float32)
    ).astype(jnp.bfloat16)
    conv_out = lon_conv(blended, lon_half[0], first_col, count_lon)
    return (middle.astype(jnp.float32) + conv_out).astype(jnp.bfloat16)[None]


BF = jnp.bfloat16
F32 = jnp.float32
MESH = pl.DeviceIdType.MESH


def norm_rows(values, gain):
    values = values.astype(F32)
    average = jnp.mean(values, axis=-1, keepdims=True)
    centered = values - average
    variance = jnp.mean(centered * centered, axis=-1, keepdims=True)
    return (centered * lax.rsqrt(variance + 1e-05) * gain).astype(BF)


def fused_kernel(
    nx, nz,
    lat_taps_h, lon_half_h, lat_half_h, quad_off_h,
    tokens_h, gain_attn_h, w_qkv_h, key_bias_h, w_out_h, gain_conv_h, w_conv_h,
    out,
    lat_taps, lon_half, lat_half, quad_off, gain_attn, w_qkv, gain_conv, w_conv, load,
    wq, wo, tok, normed, bias, bias_f, att_out, att_in, halo, other_in, mixer, mixed_all, middle,
    q_send, q_recv, o_send, o_recv, r_send, r_recv, t_send, t_recv, a_send, a_recv, h_send, h_recv, n_send, n_recv, f_send, f_recv,
    y_send, y_recv, g_send, g_recv,
):
    y, place, c = lax.axis_index("groups"), lax.axis_index("lat"), lax.axis_index("lon")
    z, x = lax.div(place, nx), lax.rem(place, nx)
    quad = y * 2 + c
    x_peer = (y, z * nx + (1 - x), c)
    z_up, z_down = (y, place + nx, c), (y, place - nx, c)
    sibling = (y, place, 1 - c)
    y_peer = (1 - y, place, c)
    diagonal = (1 - y, place, 1 - c)
    has_up, has_down = z < nz - 1, z > 0
    lat_count = nx * nz
    shard = w_qkv.shape[0]
    width = tokens_h.shape[1]
    rows = tokens_h.shape[0]
    head = 64
    part = width // 4
    half = width // 2

    barrier = pltpu.get_barrier_semaphore()

    def greet(device):
        pl.semaphore_signal(barrier, inc=1, device_id=device, device_id_type=MESH)

    for device in (x_peer, sibling, y_peer, diagonal):
        greet(device)
    for cond, device in ((has_up, z_up), (has_down, z_down)):
        @pl.when(cond)
        def _(device=device):
            greet(device)

    own_tokens = tok.at[y, pl.ds(c * rows, rows), :]
    loads = [
        pltpu.make_async_copy(source, target, load.at[k])
        for k, (source, target) in enumerate(
            (
                (w_qkv_h, w_qkv),
                (tokens_h, own_tokens),
                (gain_attn_h, gain_attn),
                (w_conv_h, w_conv),
                (key_bias_h, bias.at[c]),
                (w_out_h, wo.at[pl.ds(place * shard, shard), :]),
                (gain_conv_h, gain_conv),
                (lat_taps_h, lat_taps),
                (lon_half_h, lon_half),
                (lat_half_h, lat_half),
                (quad_off_h, quad_off),
            )
        )
    ]
    for copy in loads:
        copy.start()
    loads[0].wait()

    for pick in range(4):
        @pl.when(quad == pick)
        def _(pick=pick):
            wq[pl.ds(place * shard, shard), :] = jnp.concatenate(
                [w_qkv[:, j * width + pick * part : j * width + (pick + 1) * part] for j in range(3)],
                axis=1,
            )
    loads[1].wait()

    pl.semaphore_wait(
        barrier,
        4 + has_up.astype(jnp.int32) + has_down.astype(jnp.int32),
    )

    def remote(source, target, send, recv, device):
        return pltpu.make_async_remote_copy(
            src_ref=source, dst_ref=target, send_sem=send, recv_sem=recv,
            device_id=device, device_id_type=MESH,
        )

    def q_at(slot, h):
        return wq.at[pl.ds(slot * shard + h * (shard // 2), shard // 2), :]

    def o_at(slot, yy, cc):
        return wo.at[
            pl.ds(slot * shard + yy * (shard // 2), shard // 2), pl.ds(cc * half, half)
        ]

    class Gather:
        def __init__(self, at, send, recv, chunks):
            self.at, self.send, self.recv = at, send, recv
            self.chunks = range(chunks)

        def copy(self, slot, k, way, device, h):
            return remote(
                self.at(slot, h), self.at(slot, h),
                self.send.at[k, way, h], self.recv.at[slot, h], device,
            )

        def own(self, act):
            for h in self.chunks:
                @pl.when(has_up)
                def _(h=h):
                    act(self.copy(place, 0, 1, z_up, h))

                @pl.when(has_down)
                def _(h=h):
                    act(self.copy(place, 0, 2, z_down, h))

                act(self.copy(place, 0, 0, x_peer, h))

        def step(self, t, receive):
            act = (lambda d: d.start()) if receive else (lambda d: d.wait_send())
            for h in self.chunks:
                for sign, reach, onward, device, way, k in (
                    (-1, z >= t, has_up, z_up, 1, t),
                    (1, z + t <= nz - 1, has_down, z_down, 2, nz - 1 + t),
                ):
                    slot = (z + sign * t) * nx + x

                    @pl.when(reach)
                    def _(slot=slot, k=k, h=h):
                        if receive:
                            self.copy(slot, k, 0, x_peer, h).wait_recv()

                    @pl.when(jnp.logical_and(reach, onward))
                    def _(slot=slot, k=k, way=way, device=device, h=h):
                        act(self.copy(slot, k, way, device, h))

                    @pl.when(reach)
                    def _(slot=slot, k=k, h=h):
                        act(self.copy(slot, k, 0, x_peer, h))

        def across(self):
            for zz in range(nz):
                slot = zz * nx + (1 - x)
                for h in self.chunks:
                    self.copy(slot, 0, 0, x_peer, h).wait_recv()

        def finish(self):
            self.own(lambda d: d.wait_send())
            for t in range(1, nz):
                self.step(t, False)

    others = [(None, z * nx + (1 - x), ((has_up, 1, z_up), (has_down, 2, z_down)))]
    for t in range(1, nz):
        for sign, reach, going, way, device in (
            (-1, z >= t, has_up, 1, z_up), (1, z + t <= nz - 1, has_down, 2, z_down)
        ):
            for xx in range(nx):
                others.append(
                    (
                        reach,
                        (z + sign * t) * nx + xx,
                        ((jnp.logical_and(reach, going), way, device),),
                    )
                )

    def when(cond, run):
        if cond is None:
            run()
        else:
            pl.when(cond)(run)

    def o_copy(slot, k, way, device):
        return remote(
            o_at(slot, y, c), o_at(slot, y, c), o_send.at[k, way], o_recv.at[slot], device
        )

    def o_side(slot, k):
        return remote(o_at(slot, y, c), o_at(slot, y, c), r_send.at[k], r_recv.at[slot], sibling)

    def o_cross(slot, k):
        return remote(o_at(slot, y, c), o_at(slot, y, c), y_send.at[k], y_recv.at[slot], y_peer)

    def o_last(slot, k):
        return remote(
            o_at(slot, 1 - y, c), o_at(slot, 1 - y, c), g_send.at[k], g_recv.at[slot], sibling
        )

    def o_own(act):
        for cond, way, device in ((None, 0, x_peer), (has_up, 1, z_up), (has_down, 2, z_down)):
            when(cond, lambda way=way, device=device: act(o_copy(place, 13, way, device)))

    def o_forward(k, act):
        reach, slot, targets = others[k]
        for cond, way, device in targets:
            when(cond, lambda way=way, device=device: act(o_copy(slot, k, way, device)))

        def hand():
            act(o_cross(slot, k))
            act(o_side(slot, k))

        when(reach, hand)

    def o_step(ks):
        for k in ks:
            reach, slot, _ = others[k]
            when(reach, lambda slot=slot: o_copy(slot, 0, 0, x_peer).wait_recv())
            o_forward(k, lambda d: d.start())

    def o_collect():
        for k, (reach, slot, _) in enumerate(others):
            def run(slot=slot, k=k):
                o_cross(slot, k).wait_recv()
                o_last(slot, k).start()

            when(reach, run)
        for k, (reach, slot, _) in enumerate(others):
            def run(slot=slot, k=k):
                o_side(slot, k).wait_recv()
                o_last(slot, k).wait_recv()

            when(reach, run)

    def o_finish():
        o_own(lambda d: d.wait_send())
        for k, (reach, slot, _) in enumerate(others):
            o_forward(k, lambda d: d.wait_send())
            when(reach, lambda slot=slot, k=k: o_last(slot, k).wait_send())

    gather_q = Gather(q_at, q_send, q_recv, 2)
    start = lambda d: d.start()

    gather_q.own(start)

    def tok_at(yy, cc):
        return tok.at[yy, pl.ds(cc * rows, rows), :]

    tok_copies = [
        remote(tok_at(y, c), tok_at(y, c), t_send.at[0], t_recv.at[0], y_peer),
        remote(tok_at(y, c), tok_at(y, c), t_send.at[1], t_recv.at[1], sibling),
        remote(tok_at(1 - y, c), tok_at(1 - y, c), t_send.at[2], t_recv.at[2], sibling),
        remote(bias.at[c], bias.at[c], t_send.at[3], t_recv.at[3], sibling),
    ]
    tok_copies[0].start()
    tok_copies[1].start()
    loads[4].wait()
    tok_copies[3].start()
    loads[2].wait()
    gain_a = gain_attn[...][None]

    def norm_block(yy, cc):
        normed[yy, pl.ds(cc * rows, rows), :] = norm_rows(tok[yy, pl.ds(cc * rows, rows), :], gain_a)

    loads[5].wait()
    o_own(start)
    norm_block(y, c)
    gather_q.step(1, True)
    o_step([0])
    tok_copies[1].wait_recv()
    norm_block(y, 1 - c)
    gather_q.step(2, True)
    tok_copies[0].wait_recv()
    tok_copies[2].start()
    o_step(range(1, 5))
    gather_q.step(3, True)
    o_step(range(5, 9))
    loads[3].wait()
    pair_row = lax.broadcasted_iota(jnp.int32, (2 * head, width), 0)
    pair_col = lax.broadcasted_iota(jnp.int32, (2 * head, width), 1)
    same = lax.rem(lax.div(pair_col, head), 2) == lax.div(pair_row, head)
    for b in range(2):
        wide = jnp.concatenate([w_conv[b], w_conv[b]], axis=0).astype(F32)
        mixer[b] = jnp.where(same, wide, 0.0).astype(BF)

    norm_block(1 - y, c)
    tok_copies[2].wait_recv()
    norm_block(1 - y, 1 - c)
    tok_copies[3].wait_recv()
    bias_f[...] = jnp.concatenate([bias[0], bias[1]], axis=1).astype(F32)
    o_step(range(9, 13))
    gather_q.across()

    def att_copy(r, to_c, k, device):
        return remote(
            att_out.at[r, pl.ds(to_c * rows, rows), :], att_in.at[quad],
            a_send.at[k], a_recv.at[quad], device,
        )

    att_copies = [
        att_copy(0, c, 0, y_peer), att_copy(0, 1 - c, 1, diagonal), att_copy(1, 1 - c, 2, sibling)
    ]

    def attend(sample, r, between):
        projected = jnp.dot(normed[sample], wq[...], preferred_element_type=F32).astype(BF)
        between()
        pieces = []
        for h in range(3):
            queries = projected[:, h * head : (h + 1) * head] * jnp.asarray(head ** -0.5, BF)
            keys = projected[:, part + h * head : part + (h + 1) * head]
            vals = projected[:, 2 * part + h * head : 2 * part + (h + 1) * head]
            scores = lax.dot_general(
                queries, keys, (((1,), (1,)), ((), ())), preferred_element_type=F32
            ) + bias_f[pl.ds(quad * 3 + h, 1), :]
            expd = jnp.exp(scores - jnp.max(scores, axis=-1, keepdims=True))
            totals = jnp.sum(expd, axis=-1, keepdims=True)
            pieces.append(jnp.dot(expd.astype(BF), vals, preferred_element_type=F32) / totals)
        att_out[r] = jnp.concatenate(pieces, axis=1).astype(BF)

    attend(1 - y, 0, lambda: None)
    att_copies[0].start()
    att_copies[1].start()
    attend(y, 1, lambda: None)
    att_copies[2].start()
    att_in[quad] = att_out[1, pl.ds(c * rows, rows), :]

    o_collect()
    for source in (y * 2 + (1 - c), (1 - y) * 2 + c, (1 - y) * 2 + (1 - c)):
        remote(att_in.at[source], att_in.at[source], a_send.at[0], a_recv.at[source], sibling).wait_recv()
    branch = tok[y, pl.ds(c * rows, rows), :].astype(F32)
    for p in range(4):
        branch = branch + jnp.dot(
            att_in[p], wo[p * part : (p + 1) * part, :], preferred_element_type=F32
        )
    mid = branch.astype(BF)
    middle[...] = mid
    for k in range(6, 11):
        loads[k].wait()
    conv_in = norm_rows(mid, gain_conv[...][None])
    halo[1] = conv_in

    near, far = 2 * (1 - x), 2 * x
    passes = jnp.logical_or(jnp.logical_and(x == 0, has_up), jnp.logical_and(x == 1, has_down))
    gets = jnp.logical_or(jnp.logical_and(x == 0, has_down), jnp.logical_and(x == 1, has_up))
    onward = (y, place + nx * (1 - 2 * x), c)
    pieces = 4
    piece = rows // pieces

    def halo_at(which, k):
        return halo.at[which, pl.ds(k * piece, piece), :]

    to_near = [
        remote(halo_at(1, k), halo_at(far, k), n_send.at[k], n_recv.at[k], x_peer)
        for k in range(pieces)
    ]
    from_near = [
        remote(halo_at(1, k), halo_at(near, k), n_send.at[k], n_recv.at[k], x_peer)
        for k in range(pieces)
    ]
    to_far = [
        remote(halo_at(near, k), halo_at(far, k), f_send.at[k], f_recv.at[k], onward)
        for k in range(pieces)
    ]
    for d in to_near:
        d.start()
    to_side = remote(halo.at[1], other_in, h_send.at[2], h_recv.at[2], sibling)
    to_side.start()

    @pl.when(jnp.logical_not(gets))
    def _():
        halo[far] = jnp.zeros((rows, width), BF)

    base = quad_off[0]
    reach_lat = lat_half[0]
    wide_ok = reach_lat >= 1
    taps = [
        [
            lat_taps[b, base + r] if r == 1 else jnp.where(wide_ok, lat_taps[b, base + r], 0.0)
            for b in range(2)
        ]
        for r in range(3)
    ]
    span = (lon_half[0] + 1).astype(F32)
    limit = lon_half[0].astype(F32)
    diff = lax.broadcasted_iota(jnp.int32, (rows, rows), 1) - lax.broadcasted_iota(
        jnp.int32, (rows, rows), 0
    )

    def coeffs(offset):
        offset = offset.astype(F32)
        distance = jnp.abs(offset)
        tent = jnp.where(distance <= limit, (1.0 - distance / span) / span, 0.0)
        odd = tent * offset / span
        return jnp.concatenate([tent.astype(BF), odd.astype(BF)], axis=1)

    own_coeffs = coeffs(diff)
    side_coeffs = coeffs(jnp.where(diff >= 0, diff - rows, diff + rows))

    def mix(values, b):
        return jnp.concatenate(
            [
                lax.dot_general(
                    values[:, p * 2 * head : (p + 1) * 2 * head],
                    mixer[b, :, p * 2 * head : (p + 1) * 2 * head],
                    (((1,), (1,)), ((), ())),
                    preferred_element_type=F32,
                )
                for p in range(width // (2 * head))
            ],
            axis=1,
        ).astype(BF)

    for k in range(pieces):
        from_near[k].wait_recv()

        @pl.when(passes)
        def _(k=k):
            to_far[k].start()

    to_side.wait_recv()
    side_rows = other_in[...].astype(F32)
    polar = []
    for b in range(2):
        gain = jnp.where(place == 0, taps[0][b], 0.0) + jnp.where(
            place == lat_count - 1, taps[2][b], 0.0
        )
        polar.append(mix((gain * side_rows).astype(BF), b))

    @pl.when(gets)
    def _():
        for d in to_far:
            d.wait_recv()

    for b in range(2):
        summed = (
            taps[0][b] * halo[0].astype(F32)
            + taps[1][b] * halo[1].astype(F32)
            + taps[2][b] * halo[2].astype(F32)
        ).astype(BF)
        blended = (mix(summed, b).astype(F32) + polar[b].astype(F32)).astype(BF)
        mixed_all[c, b * rows : (b + 1) * rows, :] = blended
    to_mix = remote(mixed_all.at[c], mixed_all.at[c], h_send.at[3], h_recv.at[3], sibling)
    to_mix.start()
    total = middle[...].astype(F32) + jnp.dot(own_coeffs, mixed_all[c], preferred_element_type=F32)
    to_mix.wait_recv()
    total = total + jnp.dot(side_coeffs, mixed_all[1 - c], preferred_element_type=F32)
    out[...] = total.astype(BF)

    gather_q.finish()
    o_finish()
    for d in tok_copies + att_copies + [to_side, to_mix]:
        d.wait_send()

    for d in to_near:
        d.wait_send()

    @pl.when(passes)
    def _():
        for d in to_far:
            d.wait_send()


def fused_device(
    tokens, gain_attn, w_qkv, key_bias, w_out, gain_conv, w_conv, lat_taps, lon_half, lat_half, quad_off
):
    rows, width = tokens.shape[1:]
    shard = w_qkv.shape[0]
    heads = key_bias.shape[1]
    lat_count = width // shard
    nx = 2
    nz = lat_count // nx
    vmem = pl.BlockSpec(memory_space=pltpu.VMEM)
    anywhere = pl.BlockSpec(memory_space=pltpu.HBM)
    dma = pltpu.SemaphoreType.DMA
    kinds = 2 * nz - 1
    out = pl.pallas_call(
        lambda *refs: fused_kernel(nx, nz, *refs),
        out_shape=jax.ShapeDtypeStruct((rows, width), BF),
        in_specs=[anywhere] * 11,
        out_specs=vmem,
        scratch_shapes=[
            pltpu.SMEM((2, lat_taps.shape[0]), F32),
            pltpu.SMEM((1,), jnp.int32),
            pltpu.SMEM((1,), jnp.int32),
            pltpu.SMEM((1,), jnp.int32),
            pltpu.VMEM((width,), F32),
            pltpu.VMEM(w_qkv.shape, BF),
            pltpu.VMEM((width,), F32),
            pltpu.VMEM((2, 64, width), BF),
            dma((11,)),
            pltpu.VMEM((width, 3 * width // 4), BF),
            pltpu.VMEM((width, width), BF),
            pltpu.VMEM((2, 2 * rows, width), BF),
            pltpu.VMEM((2, 2 * rows, width), BF),
            pltpu.VMEM((2, heads, rows), BF),
            pltpu.VMEM((heads, 2 * rows), F32),
            pltpu.VMEM((2, 2 * rows, width // 4), BF),
            pltpu.VMEM((4, rows, width // 4), BF),
            pltpu.VMEM((3, rows, width), BF),
            pltpu.VMEM((rows, width), BF),
            pltpu.VMEM((2, 128, width), BF),
            pltpu.VMEM((2, 2 * rows, width), BF),
            pltpu.VMEM((rows, width), BF),
            dma((kinds, 3, 2)),
            dma((lat_count, 2)),
            dma((14, 3)),
            dma((lat_count,)),
            dma((13,)),
            dma((lat_count,)),
            dma((4,)),
            dma((4,)),
            dma((3,)),
            dma((4,)),
            dma((4,)),
            dma((4,)),
            dma((4,)),
            dma((4,)),
            dma((4,)),
            dma((4,)),
            dma((13,)),
            dma((lat_count,)),
            dma((13,)),
            dma((lat_count,)),
        ],
        compiler_params=pltpu.CompilerParams(
            collective_id=0, has_side_effects=True, vmem_limit_bytes=63 * 1024 * 1024
        ),
    )(
        lat_taps.T, lon_half, lat_half, quad_off,
        tokens[0], gain_attn, w_qkv, key_bias[0], w_out, gain_conv, jnp.swapaxes(w_conv, 1, 2),
    )
    return out[None]


def solution(mesh):
    sizes = (mesh.shape["groups"], mesh.shape["lat"], mesh.shape["lon"])
    return jax.shard_map(
        fused_device if sizes == (2, 8, 2) else per_device,
        mesh=mesh,
        in_specs=(
            P(("groups", "lat"), "lon", None),
            P(),
            P("lat", None),
            P("lat", None, "lon"),
            P("lat", None),
            P(),
            P(),
            P(),
            P("lat"),
            P("lat"),
            P("lat"),
        ),
        out_specs=P(("groups", "lat"), "lon", None),
        check_vma=False,
    )
```
